32 devices in a mesh: ctx: 8 (over z, core), exp: 4 (over y, x).
Axes of the slice: x: 2, y: 2, z: 4, core: 2. Of those that a mesh axis runs over, the one named last changes fastest.
Arguments:
- tokens: bfloat16 [16384, 1024], P(('ctx', 'exp')), may hold values from -30 to 30
- slot_keys: bfloat16 [1024, 512], replicated, may hold values from -64 to 64
- expert_in: bfloat16 [16, 1024, 2048], P('exp'), may hold values from -0.1875 to 0.1875
- expert_out: bfloat16 [16, 2048, 1024], P('exp'), may hold values from -0.25 to 0.25
- slot_counts: int32 [32, 16], P(('ctx', 'exp')), may hold values from 0 to 64, as said below
- slot_reach: int32 [32, 8], P(('ctx', 'exp')), may hold values from 0 to 7, as said below
Outputs:
- mixed: bfloat16 [16384, 1024], P(('ctx', 'exp'))
The draws below stay inside these ranges and needn't reach their ends.
Inputs may be any that keep to these rules, and one draw needn't show every extreme that they name: `slot_counts`: row k gives, in expert order, how many of the 512 slots of window k each expert takes; every row sums to 512; one expert, the same in every row, takes exactly 64 slots in every row. `slot_reach`: entry [k, j] is the last token block read by slots j * 64 to (j + 1) * 64 - 1 of window k; every row holds a 0 and a 7.
All inputs are finite; a program needn't handle non-finite values.
Results may differ from the reference program's by a relative error of at most 0.012.
The reference program's roundings to bfloat16 on the way count: a program that leaves them out, or rounds other values in their place, can miss the bound.
Values may be sent and summed in bfloat16 or wider, within the bound.
A program may use at most 64 MiB of HBM per device.

```python
import math
import jax
import jax.numpy as jnp
from jax import lax

D = 1024
HID = 2048
E = 16
BLOCK = 64
SLOTS = 512
CAP = 64
TBLK = 8
WINDOWS = 32
TOKENS = 16384


def key_parts(key):
    key_base = jax.random.fold_in(key, 0)
    return key_base


def draw_slot_keys(key, part):
    key_base = key_parts(jax.random.fold_in(key, 3))
    spread = 2.0 / math.sqrt(D)
    base = spread * jnp.clip(jax.random.normal(key_base, (D, SLOTS), jnp.float32), -6.0, 6.0)
    return jnp.clip(base, -64.0, 64.0).astype(jnp.bfloat16)


def draw_tokens(key, part):
    key_main = jax.random.fold_in(jax.random.fold_in(key, 5), 0)
    values = jnp.clip(jax.random.normal(key_main, (TOKENS, D), jnp.float32), -6.0, 6.0)
    return jnp.clip(values, -30.0, 30.0).astype(jnp.bfloat16)


def permute_experts(subkey):
    return jax.random.permutation(subkey, E)


def permute_blocks(subkey):
    return jax.random.permutation(subkey, SLOTS // BLOCK)


def draw_slot_counts(key, part):
    key_hot, key_order, key_shift = jax.random.split(jax.random.fold_in(key, 7), 3)
    hottest = jax.random.randint(key_hot, (), 0, E)
    rank_table = jax.vmap(permute_experts)(jax.random.split(key_order, WINDOWS))
    rank_table = jnp.where(jnp.arange(E)[None, :] == hottest, -1, rank_table)
    expert_order = jnp.argsort(rank_table, axis=1, stable=True)
    half_count = (E - 2) // 2
    shifts = jax.random.randint(key_shift, (WINDOWS, half_count), -(CAP // 2 - 1), CAP // 2)
    values = jnp.concatenate([jnp.full((WINDOWS, 1), CAP, jnp.int32), jnp.zeros((WINDOWS, 1), jnp.int32), (CAP // 2 + shifts).astype(jnp.int32), (CAP // 2 - shifts).astype(jnp.int32)], axis=1)
    counts = jnp.zeros((WINDOWS, E), jnp.int32).at[jnp.arange(WINDOWS)[:, None], expert_order].set(values)
    return counts.astype(jnp.int32)


def draw_slot_reach(key, part):
    key_perm, key_level = jax.random.split(jax.random.fold_in(key, 9), 2)
    placement = jax.vmap(permute_blocks)(jax.random.split(key_perm, WINDOWS))
    levels = jax.random.randint(key_level, (WINDOWS, SLOTS // BLOCK), 0, TBLK)
    return jnp.where(placement == 0, 0, jnp.where(placement == 1, TBLK - 1, levels)).astype(jnp.int32)


def block_scale(rng, extent, pieces, least, high):
    level = 1.0
    for dim, blocks in pieces:
        heights = jax.random.uniform(jax.random.fold_in(jax.random.fold_in(rng, 6), dim), (blocks,), jnp.float32, least / len(pieces), high / len(pieces))
        level = level * jnp.repeat(jnp.exp(heights), extent[dim] // blocks).reshape((-1,) + (1,) * (len(extent) - 1 - dim))
    return level


def gaussian(stream_key, shape, scale, bound, shards=(), held_as=jnp.bfloat16):
    drawn = jax.random.normal(stream_key, shape, jnp.float32) * scale
    if len(shards) > 0:
        drawn = block_scale(stream_key, shape, shards, -0.22, 0.18) * drawn
    return jnp.clip(drawn, min=-bound, max=bound).astype(held_as)


def setup_inputs(seed: int = 0) -> dict:
    key_list = jax.random.split(jax.random.key(seed), 7)
    tokens = draw_tokens(jax.random.fold_in(key_list[6], 71), 0)
    slot_keys = draw_slot_keys(jax.random.fold_in(key_list[6], 71), 0)
    expert_in = gaussian(key_list[2], (E, D, HID), D ** -0.5, 0.1875, ((0, 4),))
    expert_out = gaussian(key_list[3], (E, HID, D), (HID // 4) ** -0.5, 0.25, ((0, 4),))
    slot_counts = draw_slot_counts(jax.random.fold_in(key_list[6], 71), 0)
    slot_reach = draw_slot_reach(jax.random.fold_in(key_list[6], 71), 0)
    return dict(tokens=tokens, slot_keys=slot_keys, expert_in=expert_in, expert_out=expert_out, slot_counts=slot_counts, slot_reach=slot_reach)


EPSILON = 1e-06

def normalize(values):
    floats = values.astype(jnp.float32)
    inverse_rms = lax.rsqrt(lax.optimization_barrier(jnp.mean(floats * floats, axis=-1, keepdims=True)) + EPSILON)
    return (floats * inverse_rms).astype(jnp.bfloat16)

def block_levels(reach_row, slot_count):
    block_count = reach_row.shape[0]
    block_width = slot_count // block_count
    return jnp.broadcast_to(reach_row[:, None], (block_count, block_width)).reshape(slot_count).astype(jnp.int32)

def token_levels(tok_count):
    return (jnp.arange(tok_count, dtype=jnp.int32) // BLOCK).astype(jnp.int32)

def slot_layout(counts_row, slot_count, capacity):
    expert_count = counts_row.shape[0]
    expert_ids = jnp.arange(expert_count, dtype=jnp.int32)
    slot_ends = jnp.cumsum(counts_row).astype(jnp.int32)
    starts = (slot_ends - counts_row).astype(jnp.int32)
    slot_ids = jnp.arange(slot_count, dtype=jnp.int32)
    owner_ids = lax.optimization_barrier(jnp.sum((slot_ends[None, :] <= slot_ids[:, None]).astype(jnp.int32), axis=1)).astype(jnp.int32)
    onehot = owner_ids[:, None] == expert_ids[None, :]
    first_slot = lax.optimization_barrier(jnp.sum(jnp.where(onehot, starts[None, :], 0), axis=1)).astype(jnp.int32)
    padded_index = (owner_ids * capacity + slot_ids - first_slot).astype(jnp.int32)
    place_ids = jnp.arange(expert_count * capacity, dtype=jnp.int32)
    expert_of = (place_ids // capacity).astype(jnp.int32)
    position = (place_ids - expert_of * capacity).astype(jnp.int32)
    place_hot = expert_of[:, None] == expert_ids[None, :]
    counts_of = lax.optimization_barrier(jnp.sum(jnp.where(place_hot, counts_row[None, :], 0), axis=1)).astype(jnp.int32)
    starts_of = lax.optimization_barrier(jnp.sum(jnp.where(place_hot, starts[None, :], 0), axis=1)).astype(jnp.int32)
    is_live = position < counts_of
    source = jnp.clip(starts_of + position, 0, slot_count - 1).astype(jnp.int32)
    return (padded_index, is_live, source)

def dispatch_window(normed, slot_keys, reach_row, counts_row):
    tok_count = normed.shape[0]
    slot_count = slot_keys.shape[1]
    capacity = 2 * slot_count // counts_row.shape[0]
    logits = jnp.dot(normed.astype(jnp.float32), slot_keys.astype(jnp.float32), preferred_element_type=jnp.float32)
    allowed = token_levels(tok_count)[:, None] <= block_levels(reach_row, slot_count)[None, :]
    masked = jnp.where(allowed, logits, -jnp.inf)
    exponent = jnp.exp(masked - lax.optimization_barrier(jnp.max(masked, axis=0, keepdims=True)))
    weights = (exponent / lax.optimization_barrier(jnp.sum(exponent, axis=0, keepdims=True))).astype(jnp.bfloat16)
    slot_inputs = lax.dot_general(weights.astype(jnp.float32), normed.astype(jnp.float32), (((0,), (0,)), ((), ())), preferred_element_type=jnp.float32).astype(jnp.bfloat16)
    padded_index, is_live, source = slot_layout(counts_row, slot_count, capacity)
    packed = jnp.where(is_live[:, None], jnp.take(slot_inputs, source, axis=0), jnp.zeros((), jnp.bfloat16))
    return (logits, packed, padded_index)

def combine_window(logits, reach_row, own_out, prior_out, has_prior):
    tok_count, slot_count = logits.shape
    allowed = block_levels(reach_row, slot_count)[None, :] <= token_levels(tok_count)[:, None]
    usable = jnp.logical_or(allowed, has_prior)
    largest = lax.optimization_barrier(jnp.max(jnp.where(usable, logits, -jnp.inf), axis=1, keepdims=True))
    own_exp = jnp.exp(jnp.where(allowed, logits, -jnp.inf) - largest)
    prior_exp = jnp.exp(jnp.where(has_prior, logits, -jnp.inf) - largest)
    denominator = lax.optimization_barrier(jnp.sum(own_exp + prior_exp, axis=1, keepdims=True))
    own_weights = (own_exp / denominator).astype(jnp.bfloat16)
    prior_weights = (prior_exp / denominator).astype(jnp.bfloat16)
    summed = jnp.dot(own_weights.astype(jnp.float32), own_out.astype(jnp.float32), preferred_element_type=jnp.float32)
    summed = summed + jnp.dot(prior_weights.astype(jnp.float32), prior_out.astype(jnp.float32), preferred_element_type=jnp.float32)
    return summed.astype(jnp.bfloat16)

def expert_rows(slot_rows, w_first, w_second):
    hidden = jnp.dot(slot_rows.astype(jnp.float32), w_first.astype(jnp.float32), preferred_element_type=jnp.float32)
    hidden = jax.nn.gelu(hidden, approximate=True).astype(jnp.bfloat16)
    return jnp.dot(hidden.astype(jnp.float32), w_second.astype(jnp.float32), preferred_element_type=jnp.float32).astype(jnp.bfloat16)

def pick_rows(source_rows, positions):
    return jnp.take(source_rows, positions, axis=0)

def reference(tokens, slot_keys, expert_in, expert_out, slot_counts, slot_reach):
    windows = slot_counts.shape[0]
    experts = slot_counts.shape[1]
    model_width = tokens.shape[1]
    normed = normalize(tokens).reshape(windows, -1, model_width)

    def first_pass(members):
        return dispatch_window(members[0], slot_keys, members[1], members[2])
    logits, packed, padded_index = lax.map(first_pass, (normed, slot_reach, slot_counts))
    grouped = jnp.swapaxes(packed.reshape(windows, experts, -1, model_width), 0, 1)

    def apply_expert(members):
        slot_rows, w_first, w_second = members
        flattened = slot_rows.reshape(-1, model_width)
        return expert_rows(flattened, w_first, w_second).reshape(slot_rows.shape)
    produced = lax.map(apply_expert, (grouped, expert_in, expert_out))
    returned = jnp.swapaxes(produced, 0, 1).reshape(windows, -1, model_width)
    own_out = jax.vmap(pick_rows)(returned, padded_index)
    prior_out = jnp.concatenate([jnp.zeros_like(own_out[:1]), own_out[:-1]], axis=0)
    window_ids = jnp.arange(windows, dtype=jnp.int32)

    def second_pass(members):
        logits_window, reach_row, own_rows, prior_rows, window_id = members
        return combine_window(logits_window, reach_row, own_rows, prior_rows, window_id > 0)
    mixed = lax.map(second_pass, (logits, slot_reach, own_out, prior_out, window_ids))
    return mixed.reshape(tokens.shape)
```

```python
import functools

import jax
import jax.numpy as jnp
from jax import lax
from jax.experimental import pallas as pl
from jax.experimental.pallas import tpu as pltpu
from jax.sharding import PartitionSpec as P

BLOCK = 64
EPSILON = 1e-06
MESH = pl.DeviceIdType.MESH
ROWS = 64
LANES = 128
SHARES = (2, 2, 2, 1, 1)


def iota(shape, dim):
    return lax.broadcasted_iota(jnp.int32, shape, dim)


def dot(a, b):
    return jnp.dot(a, b, preferred_element_type=jnp.float32)


def pick(axis_ids, width, values):
    chosen = jnp.full(axis_ids.shape, values[0], jnp.int32)
    for i in range(1, len(values)):
        chosen = jnp.where(axis_ids >= i * width, values[i], chosen)
    return chosen


def chunks_of(width):
    unit = width // sum(SHARES)
    spans, at = [], 0
    for share in SHARES:
        spans.append((at, share * unit))
        at += share * unit
    return spans


def kernel(
    n_ctx, n_exp, counts, reach, tokens, keys, first, second, out,
    first_v, second_v, normed, logits, weights, slot_in, send, recv, prod, outs, place,
    mix_own, mix_peer, placed_own, placed_peer, part_send, part_recv, summed, facts, facts_s,
    weight_sem, send_in, recv_in, send_own, recv_own, send_next, recv_next,
    send_mix, recv_mix, send_part, recv_part, send_facts, recv_facts, facts_sem,
):
    toks, width = tokens.shape
    slots = keys.shape[1]
    local = first.shape[0]
    hidden = first.shape[2]
    experts = counts.shape[1]
    levels = reach.shape[1]
    cap = 2 * slots // experts
    reach_width = slots // levels
    pairs = n_exp // 2
    mine_rows = local * cap
    half = pairs * mine_rows
    spans = chunks_of(width)
    ctx, me = lax.axis_index("ctx"), lax.axis_index("exp")
    side, pair = lax.rem(me, 2), me // 2
    window = ctx * n_exp + me
    windows = n_ctx * n_exp
    partner = me + 1 - 2 * side

    def device(number):
        number = lax.rem(number + windows, windows)
        return number // n_exp, lax.rem(number, n_exp)

    def greet(barrier, where):
        pl.semaphore_signal(barrier, inc=1, device_id=where, device_id_type=MESH)

    loads = []
    for j in range(local):
        for source, target, n in ((first, first_v, 0), (second, second_v, 1)):
            load = pltpu.make_async_copy(source.at[j], target.at[j], weight_sem.at[j, n])
            load.start()
            loads.append(load)

    barrier = pltpu.get_barrier_semaphore()
    for o in range(1, n_exp):
        greet(barrier, (ctx, lax.rem(me + o, n_exp)))
    for o in (1, -1, -2):
        greet(barrier, device(window + o))

    @pl.when(pair == 0)
    def _():
        for i in range(pairs):
            greet(barrier, (lax.rem(ctx + n_ctx - 1, n_ctx), 2 * i + side))

    lane = iota((8, LANES), 1)
    row_facts = jnp.zeros((8, LANES), jnp.int32)
    for e in range(experts):
        row_facts = jnp.where(lane == e, counts[0, e], row_facts)
    for b in range(levels):
        row_facts = jnp.where(lane == experts + b, reach[0, b], row_facts)
    facts[0] = row_facts

    def normalize(i, carry):
        rows = pl.ds(pl.multiple_of(i * ROWS, ROWS), ROWS)
        floats = tokens[rows, :].astype(jnp.float32)
        scale = lax.rsqrt(jnp.mean(floats * floats, axis=-1, keepdims=True) + EPSILON)
        normed[rows, :] = (floats * scale).astype(jnp.bfloat16)
        return carry

    lax.fori_loop(0, toks // ROWS, normalize, 0)
    logits[...] = dot(normed[...], keys[...])

    slot_level = pick(iota((1, slots), 1), reach_width, [reach[0, b] for b in range(levels)])
    for b in range(slots // 128):
        cols = slice(b * 128, (b + 1) * 128)
        allowed = iota((toks, 128), 0) // BLOCK <= slot_level[:, cols]
        masked = jnp.where(allowed, logits[:, cols], -jnp.inf)
        exponent = jnp.exp(masked - jnp.max(masked, axis=0, keepdims=True))
        weights[:, cols] = (exponent / jnp.sum(exponent, axis=0, keepdims=True)).astype(jnp.bfloat16)
    slot_in[...] = lax.dot_general(
        weights[...], normed[...], (((0,), (0,)), ((), ())), preferred_element_type=jnp.float32
    ).astype(jnp.bfloat16)

    def starts_of(taken):
        starts, total = [], jnp.int32(0)
        for e in range(experts):
            starts.append(total)
            total = total + taken[e]
        return starts

    taken = [counts[0, e] for e in range(experts)]
    starts = starts_of(taken)

    pl.semaphore_wait(barrier, n_exp + 3)

    group = n_exp * cap
    mine = pl.ds(pl.multiple_of(me * cap, cap), cap)

    def tell(i, offset):
        return pltpu.make_async_remote_copy(
            src_ref=facts.at[0],
            dst_ref=facts.at[1 + i],
            send_sem=send_facts.at[i],
            recv_sem=recv_facts.at[i],
            device_id=device(window + offset),
            device_id_type=MESH,
        )

    tellings = [tell(i, offset) for i, offset in enumerate((-1, 1, 2))]
    for telling in tellings:
        telling.start()

    def to_expert(j, o):
        peer = lax.rem(me + o, n_exp)
        theirs = pl.ds(pl.multiple_of(peer * cap, cap), cap)
        return pltpu.make_async_remote_copy(
            src_ref=send.at[j, theirs],
            dst_ref=recv.at[j, mine],
            send_sem=send_in.at[j, o],
            recv_sem=recv_in.at[j, o],
            device_id=(ctx, peer),
            device_id_type=MESH,
        )

    for j in range(local):
        chosen = [d * local + j for d in range(n_exp)]
        row = iota((group, 1), 0)
        shift = pick(row, cap, [starts[e] - d * cap for d, e in enumerate(chosen)])
        limit = pick(row, cap, [taken[e] + d * cap for d, e in enumerate(chosen)])
        source = jnp.where(row < limit, row + shift, -1)
        hot = jnp.where(iota((group, slots), 1) == source, 1.0, 0.0).astype(jnp.bfloat16)
        send[j] = dot(hot, slot_in[...]).astype(jnp.bfloat16)
        for o in range(1, n_exp):
            to_expert(j, o).start()
        recv[j, mine, :] = send[j, mine, :]

    has_prior = window > 0

    def mixing(i, carry):
        rows = pl.ds(pl.multiple_of(i * ROWS, ROWS), ROWS)
        level = (iota((ROWS, slots), 0) + i * ROWS) // BLOCK
        allowed = slot_level <= level
        usable = jnp.logical_or(allowed, has_prior)
        masked = jnp.where(usable, logits[rows, :], -jnp.inf)
        every = jnp.exp(masked - jnp.max(masked, axis=1, keepdims=True))
        own = jnp.where(allowed, every, 0.0)
        prior = jnp.where(has_prior, every, 0.0)
        denominator = jnp.sum(own + prior, axis=1, keepdims=True)
        mix_own[rows, :] = (every / denominator).astype(jnp.bfloat16)
        return carry

    lax.fori_loop(0, toks // ROWS, mixing, 0)

    to_partner = pltpu.make_async_remote_copy(
        src_ref=mix_own,
        dst_ref=mix_peer,
        send_sem=send_mix,
        recv_sem=recv_mix,
        device_id=(ctx, partner),
        device_id_type=MESH,
    )
    to_partner.start()

    for telling in tellings:
        telling.wait_recv()
    fetch = pltpu.make_async_copy(facts, facts_s, facts_sem)
    fetch.start()
    fetch.wait()

    odd = side == 1
    around = {0: 0, 1: 1, -1: 2, -2: 3}
    for t in range(3):
        seen = [
            jnp.where(odd, facts_s[around[t - 2], 0, e], facts_s[around[t - 1], 0, e])
            for e in range(experts)
        ]
        begin = starts_of(seen)
        column = iota((1, half), 1)
        shifts, limits = [], []
        for b in range(pairs * local):
            i, j = b // local, b % local
            even_e, odd_e = 2 * i * local + j, (2 * i + 1) * local + j
            shifts.append(jnp.where(odd, begin[odd_e], begin[even_e]) - b * cap)
            limits.append(jnp.where(odd, seen[odd_e], seen[even_e]) + b * cap)
        source = jnp.where(column < pick(column, cap, limits), column + pick(column, cap, shifts), -1)
        place[t] = jnp.where(iota((slots, half), 0) == source, 1.0, 0.0).astype(jnp.bfloat16)

    def settle(mix, placed, prior_place, own_place, level_of_slot, some_prior):
        allowed = level_of_slot <= iota((toks, slots), 0) // BLOCK
        every = mix[...]
        prior = jnp.where(some_prior, dot(every, place[prior_place]), 0.0)
        placed[:, :half] = prior.astype(jnp.bfloat16)
        own = jnp.where(allowed, every.astype(jnp.float32), 0.0).astype(jnp.bfloat16)
        placed[:, half:] = dot(own, place[own_place]).astype(jnp.bfloat16)

    settle(mix_own, placed_own, side, 1 + side, slot_level, has_prior)
    peer_level = pick(
        iota((1, slots), 1), reach_width,
        [jnp.where(odd, facts_s[2, 0, experts + b], facts_s[1, 0, experts + b]) for b in range(levels)],
    )

    home_rows = pl.ds(pl.multiple_of(pair * mine_rows, mine_rows), mine_rows)

    def returns(unit, rows, span, o):
        target = lax.rem(pair + o, pairs)
        cols = pl.ds(*span)
        there = pl.ds(pl.multiple_of(pair * mine_rows + rows[0], cap), rows[1])
        return pltpu.make_async_remote_copy(
            src_ref=prod.at[pl.ds(2 * target, 2), pl.ds(*rows), cols],
            dst_ref=outs.at[pl.ds(1, 2), there, cols],
            send_sem=send_own.at[unit, o],
            recv_sem=recv_own.at[unit, o],
            device_id=(ctx, 2 * target + side),
            device_id_type=MESH,
        )

    def to_next(unit, rows, span, o):
        target = lax.rem(pair + o, pairs)
        cols = pl.ds(*span)
        there = pl.ds(pl.multiple_of(pair * mine_rows + rows[0], cap), rows[1])
        later = jnp.where(target == 0, 1, 0)
        return pltpu.make_async_remote_copy(
            src_ref=prod.at[lax.rem(2 * target + n_exp - 1, n_exp), pl.ds(*rows), cols],
            dst_ref=outs.at[0, there, cols],
            send_sem=send_next.at[unit, o],
            recv_sem=recv_next.at[unit, o],
            device_id=(lax.rem(ctx + later, n_ctx), 2 * target + side),
            device_id_type=MESH,
        )

    def each_copy(unit, rows, span, act):
        for o in range(1, pairs):
            act(returns(unit, rows, span, o))
            act(to_next(unit, rows, span, o))

        @pl.when(pair == 0)
        def _():
            act(to_next(unit, rows, span, 0))

    units = [(j, (j * cap, cap), 0) for j in range(local)]
    units += [(local + c - 1, (0, mine_rows), c) for c in range(1, len(spans))]

    tile = min(512, hidden)
    for j in range(local):
        loads[2 * j].wait()
        loads[2 * j + 1].wait()
        for o in range(1, n_exp):
            to_expert(j, o).wait_recv()
        total_out = None
        for t in range(hidden // tile):
            cols = slice(t * tile, (t + 1) * tile)
            active = jax.nn.gelu(dot(recv[j], first_v[j, :, cols]), approximate=True)
            term = dot(active.astype(jnp.bfloat16), second_v[j, cols, :])
            total_out = term if total_out is None else total_out + term
        prod[:, j * cap:(j + 1) * cap, :] = total_out.astype(jnp.bfloat16).reshape(n_exp, cap, width)
        unit, rows, c = units[j]
        each_copy(unit, rows, spans[c], lambda copy: copy.start())
    for unit, rows, c in units[local:]:
        each_copy(unit, rows, spans[c], lambda copy: copy.start())

    outs[pl.ds(1, 2), home_rows, :] = prod[pl.ds(2 * pair, 2), :, :]

    @pl.when(pair > 0)
    def _():
        outs[0, home_rows, :] = prod[2 * pair - 1]

    to_partner.wait_recv()
    settle(
        mix_peer, placed_peer, 1 - side, 2 - side, peer_level,
        ctx * n_exp + partner > 0,
    )

    def share(c):
        cols = pl.ds(*spans[c])
        return pltpu.make_async_remote_copy(
            src_ref=part_send.at[:, cols],
            dst_ref=part_recv.at[:, cols],
            send_sem=send_part.at[c],
            recv_sem=recv_part.at[c],
            device_id=(ctx, partner),
            device_id_type=MESH,
        )

    for c, span in enumerate(spans):
        for unit, rows, of in units:
            if of == c:
                each_copy(unit, rows, span, lambda copy: copy.wait_recv())
        cols = slice(span[0], span[0] + span[1])
        theirs = outs[pl.ds(1 - side, 2), :, cols].reshape(2 * half, span[1])
        part_send[:, cols] = dot(placed_peer[...], theirs).astype(jnp.bfloat16)
        share(c).start()
        ours = outs[pl.ds(side, 2), :, cols].reshape(2 * half, span[1])
        summed[:, cols] = dot(placed_own[...], ours)

    for c, span in enumerate(spans):
        share(c).wait_recv()
        cols = slice(span[0], span[0] + span[1])
        out[:, cols] = (summed[:, cols] + part_recv[:, cols].astype(jnp.float32)).astype(jnp.bfloat16)

    for telling in tellings:
        telling.wait_send()
    to_partner.wait_send()
    for c in range(len(spans)):
        share(c).wait_send()
    for unit, rows, c in units:
        each_copy(unit, rows, spans[c], lambda copy: copy.wait_send())
    for j in range(local):
        for o in range(1, n_exp):
            to_expert(j, o).wait_send()


def layer(n_ctx, n_exp, tokens, slot_keys, expert_in, expert_out, slot_counts, slot_reach):
    toks, width = tokens.shape
    slots = slot_keys.shape[1]
    local = expert_in.shape[0]
    experts = slot_counts.shape[1]
    cap = 2 * slots // experts
    pairs = n_exp // 2
    half = pairs * local * cap
    units = local + len(SHARES) - 1
    bf16, f32 = jnp.bfloat16, jnp.float32
    in_vmem = pl.BlockSpec(memory_space=pltpu.VMEM)
    in_smem = pl.BlockSpec(memory_space=pltpu.SMEM)
    in_any = pl.BlockSpec(memory_space=pl.ANY)
    dma = pltpu.SemaphoreType.DMA
    return pl.pallas_call(
        functools.partial(kernel, n_ctx, n_exp),
        out_shape=pltpu.VMEM((toks, width), bf16),
        in_specs=[in_smem, in_smem, in_vmem, in_vmem, in_any, in_any],
        out_specs=in_vmem,
        scratch_shapes=[
            pltpu.VMEM(expert_in.shape, bf16),
            pltpu.VMEM(expert_out.shape, bf16),
            pltpu.VMEM((toks, width), bf16),
            pltpu.VMEM((toks, slots), f32),
            pltpu.VMEM((toks, slots), bf16),
            pltpu.VMEM((slots, width), bf16),
            pltpu.VMEM((local, n_exp * cap, width), bf16),
            pltpu.VMEM((local, n_exp * cap, width), bf16),
            pltpu.VMEM((n_exp, local * cap, width), bf16),
            pltpu.VMEM((3, half, width), bf16),
            pltpu.VMEM((3, slots, half), bf16),
            pltpu.VMEM((toks, slots), bf16),
            pltpu.VMEM((toks, slots), bf16),
            pltpu.VMEM((toks, 2 * half), bf16),
            pltpu.VMEM((toks, 2 * half), bf16),
            pltpu.VMEM((toks, width), bf16),
            pltpu.VMEM((toks, width), bf16),
            pltpu.VMEM((toks, width), f32),
            pltpu.VMEM((4, 8, LANES), jnp.int32),
            pltpu.SMEM((4, 8, LANES), jnp.int32),
            dma((local, 2)),
            dma((local, n_exp)),
            dma((local, n_exp)),
            dma((units, pairs)),
            dma((units, pairs)),
            dma((units, pairs)),
            dma((units, pairs)),
            dma,
            dma,
            dma((len(SHARES),)),
            dma((len(SHARES),)),
            dma((3,)),
            dma((3,)),
            dma,
        ],
        compiler_params=pltpu.CompilerParams(
            collective_id=0, has_side_effects=True, vmem_limit_bytes=60*2**20
        ),
    )(slot_counts, slot_reach, tokens, slot_keys, expert_in, expert_out)


def solution(mesh):
    placed = (
        P(("ctx", "exp"), None),
        P(),
        P("exp", None, None),
        P("exp", None, None),
        P(("ctx", "exp"), None),
        P(("ctx", "exp"), None),
    )
    body = functools.partial(layer, mesh.shape["ctx"], mesh.shape["exp"])
    return jax.shard_map(
        body, mesh=mesh, in_specs=placed, out_specs=P(("ctx", "exp"), None), check_vma=False
    )
```

```python
import functools

import jax
import jax.numpy as jnp
from jax import lax
from jax.experimental import pallas as pl
from jax.experimental.pallas import tpu as pltpu
from jax.sharding import PartitionSpec as P

BLOCK = 64
EPSILON = 1e-06
MESH = pl.DeviceIdType.MESH
ROWS = 64
LANES = 128
SHARES = (2, 1, 1, 1, 1, 1, 1)
HALVES = 2
AHEAD = 2


def iota(shape, dim):
    return lax.broadcasted_iota(jnp.int32, shape, dim)


def dot(a, b):
    return jnp.dot(a, b, preferred_element_type=jnp.float32)


def pick(axis_ids, width, values):
    chosen = jnp.full(axis_ids.shape, values[0], jnp.int32)
    for i in range(1, len(values)):
        chosen = jnp.where(axis_ids >= i * width, values[i], chosen)
    return chosen


def chunks_of(width):
    unit = width // sum(SHARES)
    spans, at = [], 0
    for share in SHARES:
        spans.append((at, share * unit))
        at += share * unit
    return spans


def kernel(
    n_ctx, n_exp, counts, reach, tokens, keys, first, second, out,
    first_v, second_v, normed, logits, weights, slot_in, send, recv, prod, outs, place,
    mix_own, mix_peer, placed_own, placed_peer, part_send, part_recv, summed, facts, facts_s,
    weight_sem, send_in, recv_in, send_own, recv_own, send_next, recv_next,
    send_mix, recv_mix, send_part, recv_part, send_facts, recv_facts, facts_sem,
):
    toks, width = tokens.shape
    slots = keys.shape[1]
    local = first.shape[0]
    hidden = first.shape[2]
    experts = counts.shape[1]
    levels = reach.shape[1]
    cap = 2 * slots // experts
    reach_width = slots // levels
    pairs = n_exp // 2
    mine_rows = local * cap
    half = pairs * mine_rows
    spans = chunks_of(width)
    ctx, me = lax.axis_index("ctx"), lax.axis_index("exp")
    side, pair = lax.rem(me, 2), me // 2
    window = ctx * n_exp + me
    windows = n_ctx * n_exp
    partner = me + 1 - 2 * side

    def device(number):
        number = lax.rem(number + windows, windows)
        return number // n_exp, lax.rem(number, n_exp)

    def greet(barrier, where):
        pl.semaphore_signal(barrier, inc=1, device_id=where, device_id_type=MESH)

    loads = []
    for j in range(local):
        for source, target, n in ((first, first_v, 0), (second, second_v, 1)):
            load = pltpu.make_async_copy(source.at[j], target.at[j], weight_sem.at[j, n])
            load.start()
            loads.append(load)

    barrier = pltpu.get_barrier_semaphore()
    for o in range(1, n_exp):
        greet(barrier, (ctx, lax.rem(me + o, n_exp)))
    for o in (1, -1, -2):
        greet(barrier, device(window + o))

    @pl.when(pair == 0)
    def _():
        for i in range(pairs):
            greet(barrier, (lax.rem(ctx + n_ctx - 1, n_ctx), 2 * i + side))

    lane = iota((8, LANES), 1)
    row_facts = jnp.zeros((8, LANES), jnp.int32)
    for e in range(experts):
        row_facts = jnp.where(lane == e, counts[0, e], row_facts)
    for b in range(levels):
        row_facts = jnp.where(lane == experts + b, reach[0, b], row_facts)
    facts[0] = row_facts

    def normalize(i, carry):
        rows = pl.ds(pl.multiple_of(i * ROWS, ROWS), ROWS)
        floats = tokens[rows, :].astype(jnp.float32)
        scale = lax.rsqrt(jnp.mean(floats * floats, axis=-1, keepdims=True) + EPSILON)
        normed[rows, :] = (floats * scale).astype(jnp.bfloat16)
        return carry

    lax.fori_loop(0, toks // ROWS, normalize, 0)
    logits[...] = dot(normed[...], keys[...])

    slot_level = pick(iota((1, slots), 1), reach_width, [reach[0, b] for b in range(levels)])
    for b in range(slots // 128):
        cols = slice(b * 128, (b + 1) * 128)
        allowed = iota((toks, 128), 0) // BLOCK <= slot_level[:, cols]
        masked = jnp.where(allowed, logits[:, cols], -jnp.inf)
        exponent = jnp.exp(masked - jnp.max(masked, axis=0, keepdims=True))
        weights[:, cols] = (exponent / jnp.sum(exponent, axis=0, keepdims=True)).astype(jnp.bfloat16)
    slot_in[...] = lax.dot_general(
        weights[...], normed[...], (((0,), (0,)), ((), ())), preferred_element_type=jnp.float32
    ).astype(jnp.bfloat16)

    def starts_of(taken):
        starts, total = [], jnp.int32(0)
        for e in range(experts):
            starts.append(total)
            total = total + taken[e]
        return starts

    taken = [counts[0, e] for e in range(experts)]
    starts = starts_of(taken)

    pl.semaphore_wait(barrier, n_exp + 3)

    group = n_exp * cap
    mine = pl.ds(pl.multiple_of(me * cap, cap), cap)

    def tell(i, offset):
        return pltpu.make_async_remote_copy(
            src_ref=facts.at[0],
            dst_ref=facts.at[1 + i],
            send_sem=send_facts.at[i],
            recv_sem=recv_facts.at[i],
            device_id=device(window + offset),
            device_id_type=MESH,
        )

    tellings = [tell(i, offset) for i, offset in enumerate((-1, 1, 2))]
    for telling in tellings:
        telling.start()

    def to_expert(j, o):
        peer = lax.rem(me + o, n_exp)
        theirs = pl.ds(pl.multiple_of(peer * cap, cap), cap)
        return pltpu.make_async_remote_copy(
            src_ref=send.at[j, theirs],
            dst_ref=recv.at[j, mine],
            send_sem=send_in.at[j, o],
            recv_sem=recv_in.at[j, o],
            device_id=(ctx, peer),
            device_id_type=MESH,
        )

    for j in range(local):
        chosen = [d * local + j for d in range(n_exp)]
        row = iota((group, 1), 0)
        shift = pick(row, cap, [starts[e] - d * cap for d, e in enumerate(chosen)])
        limit = pick(row, cap, [taken[e] + d * cap for d, e in enumerate(chosen)])
        source = jnp.where(row < limit, row + shift, -1)
        hot = jnp.where(iota((group, slots), 1) == source, 1.0, 0.0).astype(jnp.bfloat16)
        send[j] = dot(hot, slot_in[...]).astype(jnp.bfloat16)
        for o in range(1, n_exp):
            to_expert(j, o).start()
        recv[j, mine, :] = send[j, mine, :]

    has_prior = window > 0

    def mixing(i, carry):
        rows = pl.ds(pl.multiple_of(i * ROWS, ROWS), ROWS)
        level = (iota((ROWS, slots), 0) + i * ROWS) // BLOCK
        allowed = slot_level <= level
        usable = jnp.logical_or(allowed, has_prior)
        masked = jnp.where(usable, logits[rows, :], -jnp.inf)
        every = jnp.exp(masked - jnp.max(masked, axis=1, keepdims=True))
        own = jnp.where(allowed, every, 0.0)
        prior = jnp.where(has_prior, every, 0.0)
        denominator = jnp.sum(own + prior, axis=1, keepdims=True)
        mix_own[rows, :] = (every / denominator).astype(jnp.bfloat16)
        return carry

    lax.fori_loop(0, toks // ROWS, mixing, 0)

    piece = toks // HALVES

    def to_partner(h):
        rows = pl.ds(h * piece, piece)
        return pltpu.make_async_remote_copy(
            src_ref=mix_own.at[rows],
            dst_ref=mix_peer.at[rows],
            send_sem=send_mix.at[h],
            recv_sem=recv_mix.at[h],
            device_id=(ctx, partner),
            device_id_type=MESH,
        )

    for h in range(HALVES):
        to_partner(h).start()

    for telling in tellings:
        telling.wait_recv()
    fetch = pltpu.make_async_copy(facts, facts_s, facts_sem)
    fetch.start()
    fetch.wait()

    odd = side == 1
    around = {0: 0, 1: 1, -1: 2, -2: 3}
    for t in range(3):
        seen = [
            jnp.where(odd, facts_s[around[t - 2], 0, e], facts_s[around[t - 1], 0, e])
            for e in range(experts)
        ]
        begin = starts_of(seen)
        column = iota((1, half), 1)
        shifts, limits = [], []
        for b in range(pairs * local):
            i, j = b // local, b % local
            even_e, odd_e = 2 * i * local + j, (2 * i + 1) * local + j
            shifts.append(jnp.where(odd, begin[odd_e], begin[even_e]) - b * cap)
            limits.append(jnp.where(odd, seen[odd_e], seen[even_e]) + b * cap)
        source = jnp.where(column < pick(column, cap, limits), column + pick(column, cap, shifts), -1)
        place[t] = jnp.where(iota((slots, half), 0) == source, 1.0, 0.0).astype(jnp.bfloat16)

    def settle(h, mix, placed, prior_place, own_place, level_of_slot, some_prior):
        rows = slice(h * piece, (h + 1) * piece)
        allowed = level_of_slot <= (iota((piece, slots), 0) + h * piece) // BLOCK
        every = mix[rows, :]
        prior = jnp.where(some_prior, dot(every, place[prior_place]), 0.0)
        placed[rows, :half] = prior.astype(jnp.bfloat16)
        own = jnp.where(allowed, every.astype(jnp.float32), 0.0).astype(jnp.bfloat16)
        placed[rows, half:] = dot(own, place[own_place]).astype(jnp.bfloat16)

    for h in range(HALVES):
        settle(h, mix_own, placed_own, side, 1 + side, slot_level, has_prior)
    peer_level = pick(
        iota((1, slots), 1), reach_width,
        [jnp.where(odd, facts_s[2, 0, experts + b], facts_s[1, 0, experts + b]) for b in range(levels)],
    )

    home_rows = pl.ds(pl.multiple_of(pair * mine_rows, mine_rows), mine_rows)

    def returns(unit, rows, span, o):
        target = lax.rem(pair + o, pairs)
        cols = pl.ds(*span)
        there = pl.ds(pl.multiple_of(pair * mine_rows + rows[0], cap), rows[1])
        return pltpu.make_async_remote_copy(
            src_ref=prod.at[pl.ds(2 * target, 2), pl.ds(*rows), cols],
            dst_ref=outs.at[pl.ds(1, 2), there, cols],
            send_sem=send_own.at[unit, o],
            recv_sem=recv_own.at[unit, o],
            device_id=(ctx, 2 * target + side),
            device_id_type=MESH,
        )

    def to_next(unit, rows, span, o):
        target = lax.rem(pair + o, pairs)
        cols = pl.ds(*span)
        there = pl.ds(pl.multiple_of(pair * mine_rows + rows[0], cap), rows[1])
        later = jnp.where(target == 0, 1, 0)
        return pltpu.make_async_remote_copy(
            src_ref=prod.at[lax.rem(2 * target + n_exp - 1, n_exp), pl.ds(*rows), cols],
            dst_ref=outs.at[0, there, cols],
            send_sem=send_next.at[unit, o],
            recv_sem=recv_next.at[unit, o],
            device_id=(lax.rem(ctx + later, n_ctx), 2 * target + side),
            device_id_type=MESH,
        )

    def each_return(unit, rows, c, act):
        for o in range(1, pairs):
            act(returns(unit, rows, spans[c], o))

    def each_next(unit, rows, c, act):
        for o in range(1, pairs):
            act(to_next(unit, rows, spans[c], o))

        @pl.when(pair == 0)
        def _():
            act(to_next(unit, rows, spans[c], 0))

    def send_back(unit):
        each_next(*unit, lambda copy: copy.start())
        each_return(*unit, lambda copy: copy.start())

    units = [(j, (j * cap, cap), 0) for j in range(local)]
    units += [(local + c - 1, (0, mine_rows), c) for c in range(1, len(spans))]

    tile = min(512, hidden)
    for j in range(local):
        loads[2 * j].wait()
        loads[2 * j + 1].wait()
        for o in range(1, n_exp):
            to_expert(j, o).wait_recv()
        total_out = None
        for t in range(hidden // tile):
            cols = slice(t * tile, (t + 1) * tile)
            active = jax.nn.gelu(dot(recv[j], first_v[j, :, cols]), approximate=True)
            term = dot(active.astype(jnp.bfloat16), second_v[j, cols, :])
            total_out = term if total_out is None else total_out + term
        prod[:, j * cap:(j + 1) * cap, :] = total_out.astype(jnp.bfloat16).reshape(n_exp, cap, width)
        send_back(units[j])
    for unit in units[local:local + AHEAD - 1]:
        send_back(unit)

    outs[pl.ds(1, 2), home_rows, :] = prod[pl.ds(2 * pair, 2), :, :]

    @pl.when(pair > 0)
    def _():
        outs[0, home_rows, :] = prod[2 * pair - 1]

    shares = [(c, h * piece, piece) for c in range(1) for h in range(HALVES)]
    shares += [(c, 0, toks) for c in range(1, len(spans))]

    def share(n):
        c, at, size = shares[n]
        rows, cols = pl.ds(at, size), pl.ds(*spans[c])
        return pltpu.make_async_remote_copy(
            src_ref=part_send.at[rows, cols],
            dst_ref=part_recv.at[rows, cols],
            send_sem=send_part.at[n],
            recv_sem=recv_part.at[n],
            device_id=(ctx, partner),
            device_id_type=MESH,
        )

    def returned(c):
        for unit in units:
            if unit[2] == c:
                each_return(*unit, lambda copy: copy.wait_recv())
                each_next(*unit, lambda copy: copy.wait_recv())

    for n, (c, at, size) in enumerate(shares):
        cols = slice(spans[c][0], spans[c][0] + spans[c][1])
        rows = slice(at, at + size)
        if at == 0:
            returned(c)
            if c + AHEAD < len(spans):
                send_back(units[local + c + AHEAD - 1])
        if c == 0:
            to_partner(n).wait_recv()
            settle(
                n, mix_peer, placed_peer, 1 - side, 2 - side, peer_level,
                ctx * n_exp + partner > 0,
            )
        theirs = outs[pl.ds(1 - side, 2), :, cols].reshape(2 * half, spans[c][1])
        part_send[rows, cols] = dot(placed_peer[rows, :], theirs).astype(jnp.bfloat16)
        share(n).start()
        if at + size == toks:
            ours = outs[pl.ds(side, 2), :, cols].reshape(2 * half, spans[c][1])
            summed[:, cols] = dot(placed_own[...], ours)

    for n, (c, at, size) in enumerate(shares):
        share(n).wait_recv()
        cols = slice(spans[c][0], spans[c][0] + spans[c][1])
        rows = slice(at, at + size)
        received = part_recv[rows, cols].astype(jnp.float32)
        out[rows, cols] = (summed[rows, cols] + received).astype(jnp.bfloat16)

    for telling in tellings:
        telling.wait_send()
    for h in range(HALVES):
        to_partner(h).wait_send()
    for n in range(len(shares)):
        share(n).wait_send()
    for unit in units:
        each_return(*unit, lambda copy: copy.wait_send())
        each_next(*unit, lambda copy: copy.wait_send())
    for j in range(local):
        for o in range(1, n_exp):
            to_expert(j, o).wait_send()


def layer(n_ctx, n_exp, tokens, slot_keys, expert_in, expert_out, slot_counts, slot_reach):
    toks, width = tokens.shape
    slots = slot_keys.shape[1]
    local = expert_in.shape[0]
    experts = slot_counts.shape[1]
    cap = 2 * slots // experts
    pairs = n_exp // 2
    half = pairs * local * cap
    units = local + len(SHARES) - 1
    bf16, f32 = jnp.bfloat16, jnp.float32
    in_vmem = pl.BlockSpec(memory_space=pltpu.VMEM)
    in_smem = pl.BlockSpec(memory_space=pltpu.SMEM)
    in_any = pl.BlockSpec(memory_space=pl.ANY)
    dma = pltpu.SemaphoreType.DMA
    return pl.pallas_call(
        functools.partial(kernel, n_ctx, n_exp),
        out_shape=pltpu.VMEM((toks, width), bf16),
        in_specs=[in_smem, in_smem, in_vmem, in_vmem, in_any, in_any],
        out_specs=in_vmem,
        scratch_shapes=[
            pltpu.VMEM(expert_in.shape, bf16),
            pltpu.VMEM(expert_out.shape, bf16),
            pltpu.VMEM((toks, width), bf16),
            pltpu.VMEM((toks, slots), f32),
            pltpu.VMEM((toks, slots), bf16),
            pltpu.VMEM((slots, width), bf16),
            pltpu.VMEM((local, n_exp * cap, width), bf16),
            pltpu.VMEM((local, n_exp * cap, width), bf16),
            pltpu.VMEM((n_exp, local * cap, width), bf16),
            pltpu.VMEM((3, half, width), bf16),
            pltpu.VMEM((3, slots, half), bf16),
            pltpu.VMEM((toks, slots), bf16),
            pltpu.VMEM((toks, slots), bf16),
            pltpu.VMEM((toks, 2 * half), bf16),
            pltpu.VMEM((toks, 2 * half), bf16),
            pltpu.VMEM((toks, width), bf16),
            pltpu.VMEM((toks, width), bf16),
            pltpu.VMEM((toks, width), f32),
            pltpu.VMEM((4, 8, LANES), jnp.int32),
            pltpu.SMEM((4, 8, LANES), jnp.int32),
            dma((local, 2)),
            dma((local, n_exp)),
            dma((local, n_exp)),
            dma((units, pairs)),
            dma((units, pairs)),
            dma((units, pairs)),
            dma((units, pairs)),
            dma((HALVES,)),
            dma((HALVES,)),
            dma((len(SHARES) + HALVES,)),
            dma((len(SHARES) + HALVES,)),
            dma((3,)),
            dma((3,)),
            dma,
        ],
        compiler_params=pltpu.CompilerParams(
            collective_id=0, has_side_effects=True, vmem_limit_bytes=60*2**20
        ),
    )(slot_counts, slot_reach, tokens, slot_keys, expert_in, expert_out)


def solution(mesh):
    placed = (
        P(("ctx", "exp"), None),
        P(),
        P("exp", None, None),
        P("exp", None, None),
        P(("ctx", "exp"), None),
        P(("ctx", "exp"), None),
    )
    body = functools.partial(layer, mesh.shape["ctx"], mesh.shape["exp"])
    return jax.shard_map(
        body, mesh=mesh, in_specs=placed, out_specs=P(("ctx", "exp"), None), check_vma=False
    )
```

```python
import functools

import jax
import jax.numpy as jnp
from jax import lax
from jax.experimental import pallas as pl
from jax.experimental.pallas import tpu as pltpu
from jax.sharding import PartitionSpec as P

BLOCK = 64
EPSILON = 1e-06
MESH = pl.DeviceIdType.MESH
ROWS = 64
LANES = 128
SHARES = (2, 1, 1, 1, 1, 1, 1)
HALVES = 2
AHEAD = 2
NEXT_AHEAD = 3
OFFSETS = (-1, 1, 2)


def iota(shape, dim):
    return lax.broadcasted_iota(jnp.int32, shape, dim)


def dot(a, b):
    return jnp.dot(a, b, preferred_element_type=jnp.float32)


def pick(axis_ids, width, values):
    chosen = jnp.full(axis_ids.shape, values[0], jnp.int32)
    for i in range(1, len(values)):
        chosen = jnp.where(axis_ids >= i * width, values[i], chosen)
    return chosen


def chunks_of(width):
    unit = width // sum(SHARES)
    spans, at = [], 0
    for share in SHARES:
        spans.append((at, share * unit))
        at += share * unit
    return spans


def kernel(
    n_ctx, n_exp, counts, reach, tokens, keys, first, second, out,
    tokens_v, keys_v, first_v, second_v, normed, logits, weights, slot_in, send, recv, prod, outs, place,
    mix_own, mix_peer, placed_own, placed_peer, part_send, part_recv, summed, facts, facts_s,
    token_sem, key_sem, weight_sem, send_in, recv_in, send_own, recv_own, send_next, recv_next,
    send_mix, recv_mix, send_part, recv_part, send_facts, recv_facts, facts_sem,
):
    toks, width = tokens.shape
    slots = keys.shape[1]
    local = first.shape[0]
    hidden = first.shape[2]
    experts = counts.shape[1]
    levels = reach.shape[1]
    cap = 2 * slots // experts
    reach_width = slots // levels
    pairs = n_exp // 2
    mine_rows = local * cap
    half = pairs * mine_rows
    spans = chunks_of(width)
    ctx, me = lax.axis_index("ctx"), lax.axis_index("exp")
    side, pair = lax.rem(me, 2), me // 2
    window = ctx * n_exp + me
    windows = n_ctx * n_exp
    partner = me + 1 - 2 * side

    def device(number):
        number = lax.rem(number + windows, windows)
        return number // n_exp, lax.rem(number, n_exp)

    def exists(number):
        return jnp.logical_and(number >= 0, number < windows)

    def greet(barrier, where):
        pl.semaphore_signal(barrier, inc=1, device_id=where, device_id_type=MESH)

    piece = toks // HALVES
    token_loads = []
    for h in range(HALVES):
        rows = pl.ds(h * piece, piece)
        token_loads.append(pltpu.make_async_copy(tokens.at[rows], tokens_v.at[rows], token_sem.at[h]))
    key_load = pltpu.make_async_copy(keys, keys_v, key_sem)
    for load in token_loads:
        load.start()
    key_load.start()

    facts[...] = jnp.zeros(facts.shape, jnp.int32)
    barrier = pltpu.get_barrier_semaphore()
    for o in range(1, n_exp):
        greet(barrier, (ctx, lax.rem(me + o, n_exp)))
    for o in (-2, -1, 1):
        @pl.when(exists(window + o))
        def _(o=o):
            greet(barrier, device(window + o))

    @pl.when(jnp.logical_and(pair == 0, ctx > 0))
    def _():
        for i in range(pairs):
            greet(barrier, (ctx - 1, 2 * i + side))

    lane = iota((8, LANES), 1)
    row_facts = jnp.zeros((8, LANES), jnp.int32)
    for e in range(experts):
        row_facts = jnp.where(lane == e, counts[0, e], row_facts)
    for b in range(levels):
        row_facts = jnp.where(lane == experts + b, reach[0, b], row_facts)
    facts[0] = row_facts

    def normalize(at):
        rows = slice(at, at + ROWS)
        floats = tokens_v[rows, :].astype(jnp.float32)
        scale = lax.rsqrt(jnp.mean(floats * floats, axis=-1, keepdims=True) + EPSILON)
        normed[rows, :] = (floats * scale).astype(jnp.bfloat16)

    for h in range(HALVES):
        token_loads[h].wait()
        for at in range(h * piece, (h + 1) * piece, ROWS):
            normalize(at)
        if h == 0:
            key_load.wait()
        rows = slice(h * piece, (h + 1) * piece)
        logits[rows, :] = dot(normed[rows, :], keys_v[...])

    loads = []
    for j in range(local):
        for source, target, n in ((first, first_v, 0), (second, second_v, 1)):
            load = pltpu.make_async_copy(source.at[j], target.at[j], weight_sem.at[j, n])
            load.start()
            loads.append(load)

    slot_level = pick(iota((1, slots), 1), reach_width, [reach[0, b] for b in range(levels)])
    for b in range(slots // 128):
        cols = slice(b * 128, (b + 1) * 128)
        allowed = iota((toks, 128), 0) // BLOCK <= slot_level[:, cols]
        masked = jnp.where(allowed, logits[:, cols], -jnp.inf)
        exponent = jnp.exp(masked - jnp.max(masked, axis=0, keepdims=True))
        weights[:, cols] = (exponent / jnp.sum(exponent, axis=0, keepdims=True)).astype(jnp.bfloat16)
    slot_in[...] = lax.dot_general(
        weights[...], normed[...], (((0,), (0,)), ((), ())), preferred_element_type=jnp.float32
    ).astype(jnp.bfloat16)

    def starts_of(taken):
        starts, total = [], jnp.int32(0)
        for e in range(experts):
            starts.append(total)
            total = total + taken[e]
        return starts

    taken = [counts[0, e] for e in range(experts)]
    starts = starts_of(taken)

    told = sum(jnp.where(exists(window + o), 1, 0) for o in OFFSETS)
    pl.semaphore_wait(barrier, n_exp - 1 + told + jnp.where(ctx < n_ctx - 1, 1, 0))

    group = n_exp * cap
    mine = pl.ds(pl.multiple_of(me * cap, cap), cap)

    def tell(i, offset):
        return pltpu.make_async_remote_copy(
            src_ref=facts.at[0],
            dst_ref=facts.at[1 + i],
            send_sem=send_facts.at[i],
            recv_sem=recv_facts.at[i],
            device_id=device(window + offset),
            device_id_type=MESH,
        )

    for i, offset in enumerate(OFFSETS):
        @pl.when(exists(window + offset))
        def _(i=i, offset=offset):
            tell(i, offset).start()

    def to_expert(j, o):
        peer = lax.rem(me + o, n_exp)
        theirs = pl.ds(pl.multiple_of(peer * cap, cap), cap)
        return pltpu.make_async_remote_copy(
            src_ref=send.at[j, theirs],
            dst_ref=recv.at[j, mine],
            send_sem=send_in.at[j, o],
            recv_sem=recv_in.at[j, o],
            device_id=(ctx, peer),
            device_id_type=MESH,
        )

    for j in range(local):
        chosen = [d * local + j for d in range(n_exp)]
        row = iota((group, 1), 0)
        shift = pick(row, cap, [starts[e] - d * cap for d, e in enumerate(chosen)])
        limit = pick(row, cap, [taken[e] + d * cap for d, e in enumerate(chosen)])
        source = jnp.where(row < limit, row + shift, -1)
        hot = jnp.where(iota((group, slots), 1) == source, 1.0, 0.0).astype(jnp.bfloat16)
        send[j] = dot(hot, slot_in[...]).astype(jnp.bfloat16)
        for o in range(1, n_exp):
            to_expert(j, o).start()
        recv[j, mine, :] = send[j, mine, :]

    has_prior = window > 0

    def mixing(i, carry):
        rows = pl.ds(pl.multiple_of(i * ROWS, ROWS), ROWS)
        level = (iota((ROWS, slots), 0) + i * ROWS) // BLOCK
        allowed = slot_level <= level
        usable = jnp.logical_or(allowed, has_prior)
        masked = jnp.where(usable, logits[rows, :], -jnp.inf)
        every = jnp.exp(masked - jnp.max(masked, axis=1, keepdims=True))
        own = jnp.where(allowed, every, 0.0)
        prior = jnp.where(has_prior, every, 0.0)
        denominator = jnp.sum(own + prior, axis=1, keepdims=True)
        mix_own[rows, :] = (every / denominator).astype(jnp.bfloat16)
        return carry

    lax.fori_loop(0, toks // ROWS, mixing, 0)

    def to_partner(h):
        rows = pl.ds(h * piece, piece)
        return pltpu.make_async_remote_copy(
            src_ref=mix_own.at[rows],
            dst_ref=mix_peer.at[rows],
            send_sem=send_mix.at[h],
            recv_sem=recv_mix.at[h],
            device_id=(ctx, partner),
            device_id_type=MESH,
        )

    for h in range(HALVES):
        to_partner(h).start()

    for i, offset in enumerate(OFFSETS):
        @pl.when(exists(window - offset))
        def _(i=i, offset=offset):
            tell(i, offset).wait_recv()
    fetch = pltpu.make_async_copy(facts, facts_s, facts_sem)
    fetch.start()
    fetch.wait()

    odd = side == 1
    around = {0: 0, 1: 1, -1: 2, -2: 3}
    for t in range(3):
        seen = [
            jnp.where(odd, facts_s[around[t - 2], 0, e], facts_s[around[t - 1], 0, e])
            for e in range(experts)
        ]
        begin = starts_of(seen)
        column = iota((1, half), 1)
        shifts, limits = [], []
        for b in range(pairs * local):
            i, j = b // local, b % local
            even_e, odd_e = 2 * i * local + j, (2 * i + 1) * local + j
            shifts.append(jnp.where(odd, begin[odd_e], begin[even_e]) - b * cap)
            limits.append(jnp.where(odd, seen[odd_e], seen[even_e]) + b * cap)
        source = jnp.where(column < pick(column, cap, limits), column + pick(column, cap, shifts), -1)
        place[t] = jnp.where(iota((slots, half), 0) == source, 1.0, 0.0).astype(jnp.bfloat16)

    def settle(h, mix, placed, prior_place, own_place, level_of_slot, some_prior):
        rows = slice(h * piece, (h + 1) * piece)
        allowed = level_of_slot <= (iota((piece, slots), 0) + h * piece) // BLOCK
        every = mix[rows, :]
        prior = jnp.where(some_prior, dot(every, place[prior_place]), 0.0)
        placed[rows, :half] = prior.astype(jnp.bfloat16)
        own = jnp.where(allowed, every.astype(jnp.float32), 0.0).astype(jnp.bfloat16)
        placed[rows, half:] = dot(own, place[own_place]).astype(jnp.bfloat16)

    for h in range(HALVES):
        settle(h, mix_own, placed_own, side, 1 + side, slot_level, has_prior)
    peer_level = pick(
        iota((1, slots), 1), reach_width,
        [jnp.where(odd, facts_s[2, 0, experts + b], facts_s[1, 0, experts + b]) for b in range(levels)],
    )

    home_rows = pl.ds(pl.multiple_of(pair * mine_rows, mine_rows), mine_rows)

    def returns(unit, rows, span, o):
        target = lax.rem(pair + o, pairs)
        cols = pl.ds(*span)
        there = pl.ds(pl.multiple_of(pair * mine_rows + rows[0], cap), rows[1])
        return pltpu.make_async_remote_copy(
            src_ref=prod.at[pl.ds(2 * target, 2), pl.ds(*rows), cols],
            dst_ref=outs.at[pl.ds(1, 2), there, cols],
            send_sem=send_own.at[unit, o],
            recv_sem=recv_own.at[unit, o],
            device_id=(ctx, 2 * target + side),
            device_id_type=MESH,
        )

    def to_next(unit, rows, span, o):
        target = lax.rem(pair + o, pairs)
        cols = pl.ds(*span)
        there = pl.ds(pl.multiple_of(pair * mine_rows + rows[0], cap), rows[1])
        later = jnp.where(target == 0, 1, 0)
        return pltpu.make_async_remote_copy(
            src_ref=prod.at[lax.rem(2 * target + n_exp - 1, n_exp), pl.ds(*rows), cols],
            dst_ref=outs.at[0, there, cols],
            send_sem=send_next.at[unit, o],
            recv_sem=recv_next.at[unit, o],
            device_id=(lax.rem(ctx + later, n_ctx), 2 * target + side),
            device_id_type=MESH,
        )

    def each_return(unit, rows, c, act):
        for o in range(1, pairs):
            act(returns(unit, rows, spans[c], o))

    more, earlier = ctx < n_ctx - 1, ctx > 0

    def each_next(unit, rows, c, act, arriving=False):
        for o in range(pairs):
            first_of = pair == 0 if arriving else lax.rem(pair + o, pairs) == 0
            across = jnp.logical_and(first_of, earlier if arriving else more)
            needed = across if o == 0 else jnp.logical_or(jnp.logical_not(first_of), across)

            @pl.when(needed)
            def _(o=o):
                act(to_next(unit, rows, spans[c], o))

    def pass_on(unit):
        each_next(*unit, lambda copy: copy.start())

    def send_back(unit):
        each_return(*unit, lambda copy: copy.start())

    units = [(j, (j * cap, cap), 0) for j in range(local)]
    units += [(local + c - 1, (0, mine_rows), c) for c in range(1, len(spans))]

    tile = min(512, hidden)
    for j in range(local):
        loads[2 * j].wait()
        loads[2 * j + 1].wait()
        for o in range(1, n_exp):
            to_expert(j, o).wait_recv()
        total_out = None
        for t in range(hidden // tile):
            cols = slice(t * tile, (t + 1) * tile)
            active = jax.nn.gelu(dot(recv[j], first_v[j, :, cols]), approximate=True)
            term = dot(active.astype(jnp.bfloat16), second_v[j, cols, :])
            total_out = term if total_out is None else total_out + term
        prod[:, j * cap:(j + 1) * cap, :] = total_out.astype(jnp.bfloat16).reshape(n_exp, cap, width)
        pass_on(units[j])
        send_back(units[j])
    for ahead in range(1, max(AHEAD, NEXT_AHEAD)):
        if ahead < NEXT_AHEAD:
            pass_on(units[local + ahead - 1])
        if ahead < AHEAD:
            send_back(units[local + ahead - 1])

    outs[pl.ds(1, 2), home_rows, :] = prod[pl.ds(2 * pair, 2), :, :]

    @pl.when(pair > 0)
    def _():
        outs[0, home_rows, :] = prod[2 * pair - 1]

    @pl.when(jnp.logical_and(pair == 0, ctx == 0))
    def _():
        outs[0] = jnp.zeros(outs.shape[1:], jnp.bfloat16)

    shares = [(c, h * piece, piece) for c in range(1) for h in range(HALVES)]
    shares += [(c, 0, toks) for c in range(1, len(spans))]

    def share(n):
        c, at, size = shares[n]
        rows, cols = pl.ds(at, size), pl.ds(*spans[c])
        return pltpu.make_async_remote_copy(
            src_ref=part_send.at[rows, cols],
            dst_ref=part_recv.at[rows, cols],
            send_sem=send_part.at[n],
            recv_sem=recv_part.at[n],
            device_id=(ctx, partner),
            device_id_type=MESH,
        )

    def returned(c):
        for unit in units:
            if unit[2] == c:
                each_return(*unit, lambda copy: copy.wait_recv())
                each_next(*unit, lambda copy: copy.wait_recv(), arriving=True)

    for n, (c, at, size) in enumerate(shares):
        cols = slice(spans[c][0], spans[c][0] + spans[c][1])
        rows = slice(at, at + size)
        if at == 0:
            returned(c)
            if c + NEXT_AHEAD < len(spans):
                pass_on(units[local + c + NEXT_AHEAD - 1])
            if c + AHEAD < len(spans):
                send_back(units[local + c + AHEAD - 1])
        if c == 0:
            to_partner(n).wait_recv()
            settle(
                n, mix_peer, placed_peer, 1 - side, 2 - side, peer_level,
                ctx * n_exp + partner > 0,
            )
        theirs = outs[pl.ds(1 - side, 2), :, cols].reshape(2 * half, spans[c][1])
        part_send[rows, cols] = dot(placed_peer[rows, :], theirs).astype(jnp.bfloat16)
        share(n).start()
        if at + size == toks:
            ours = outs[pl.ds(side, 2), :, cols].reshape(2 * half, spans[c][1])
            summed[:, cols] = dot(placed_own[...], ours)

    for n, (c, at, size) in enumerate(shares):
        share(n).wait_recv()
        cols = slice(spans[c][0], spans[c][0] + spans[c][1])
        rows = slice(at, at + size)
        received = part_recv[rows, cols].astype(jnp.float32)
        out[rows, cols] = (summed[rows, cols] + received).astype(jnp.bfloat16)

    for i, offset in enumerate(OFFSETS):
        @pl.when(exists(window + offset))
        def _(i=i, offset=offset):
            tell(i, offset).wait_send()
    for h in range(HALVES):
        to_partner(h).wait_send()
    for n in range(len(shares)):
        share(n).wait_send()
    for unit in units:
        each_return(*unit, lambda copy: copy.wait_send())
        each_next(*unit, lambda copy: copy.wait_send())
    for j in range(local):
        for o in range(1, n_exp):
            to_expert(j, o).wait_send()


def layer(n_ctx, n_exp, tokens, slot_keys, expert_in, expert_out, slot_counts, slot_reach):
    toks, width = tokens.shape
    slots = slot_keys.shape[1]
    local = expert_in.shape[0]
    experts = slot_counts.shape[1]
    cap = 2 * slots // experts
    pairs = n_exp // 2
    half = pairs * local * cap
    units = local + len(SHARES) - 1
    bf16, f32 = jnp.bfloat16, jnp.float32
    in_vmem = pl.BlockSpec(memory_space=pltpu.VMEM)
    in_smem = pl.BlockSpec(memory_space=pltpu.SMEM)
    in_any = pl.BlockSpec(memory_space=pl.ANY)
    dma = pltpu.SemaphoreType.DMA
    return pl.pallas_call(
        functools.partial(kernel, n_ctx, n_exp),
        out_shape=pltpu.VMEM((toks, width), bf16),
        in_specs=[in_smem, in_smem, in_any, in_any, in_any, in_any],
        out_specs=in_vmem,
        scratch_shapes=[
            pltpu.VMEM((toks, width), bf16),
            pltpu.VMEM(slot_keys.shape, bf16),
            pltpu.VMEM(expert_in.shape, bf16),
            pltpu.VMEM(expert_out.shape, bf16),
            pltpu.VMEM((toks, width), bf16),
            pltpu.VMEM((toks, slots), f32),
            pltpu.VMEM((toks, slots), bf16),
            pltpu.VMEM((slots, width), bf16),
            pltpu.VMEM((local, n_exp * cap, width), bf16),
            pltpu.VMEM((local, n_exp * cap, width), bf16),
            pltpu.VMEM((n_exp, local * cap, width), bf16),
            pltpu.VMEM((3, half, width), bf16),
            pltpu.VMEM((3, slots, half), bf16),
            pltpu.VMEM((toks, slots), bf16),
            pltpu.VMEM((toks, slots), bf16),
            pltpu.VMEM((toks, 2 * half), bf16),
            pltpu.VMEM((toks, 2 * half), bf16),
            pltpu.VMEM((toks, width), bf16),
            pltpu.VMEM((toks, width), bf16),
            pltpu.VMEM((toks, width), f32),
            pltpu.VMEM((4, 8, LANES), jnp.int32),
            pltpu.SMEM((4, 8, LANES), jnp.int32),
            dma((HALVES,)),
            dma,
            dma((local, 2)),
            dma((local, n_exp)),
            dma((local, n_exp)),
            dma((units, pairs)),
            dma((units, pairs)),
            dma((units, pairs)),
            dma((units, pairs)),
            dma((HALVES,)),
            dma((HALVES,)),
            dma((len(SHARES) + HALVES,)),
            dma((len(SHARES) + HALVES,)),
            dma((3,)),
            dma((3,)),
            dma,
        ],
        compiler_params=pltpu.CompilerParams(
            collective_id=0, has_side_effects=True, vmem_limit_bytes=60*2**20
        ),
    )(slot_counts, slot_reach, tokens, slot_keys, expert_in, expert_out)


def solution(mesh):
    placed = (
        P(("ctx", "exp"), None),
        P(),
        P("exp", None, None),
        P("exp", None, None),
        P(("ctx", "exp"), None),
        P(("ctx", "exp"), None),
    )
    body = functools.partial(layer, mesh.shape["ctx"], mesh.shape["exp"])
    return jax.shard_map(
        body, mesh=mesh, in_specs=placed, out_specs=P(("ctx", "exp"), None), check_vma=False
    )
```

```python
import functools

import jax
import jax.numpy as jnp
from jax import lax
from jax.experimental import pallas as pl
from jax.experimental.pallas import tpu as pltpu
from jax.sharding import PartitionSpec as P

BLOCK = 64
EPSILON = 1e-06
MESH = pl.DeviceIdType.MESH
ROWS = 64
LANES = 128
SHARES = (2, 1, 1, 1, 1, 1, 1)
HALVES = 2
LEADS = (3, 5)
OFFSETS = (-1, 1, 2)


def iota(shape, dim):
    return lax.broadcasted_iota(jnp.int32, shape, dim)


def dot(a, b):
    return jnp.dot(a, b, preferred_element_type=jnp.float32)


def pick(axis_ids, width, values):
    chosen = jnp.full(axis_ids.shape, values[0], jnp.int32)
    for i in range(1, len(values)):
        chosen = jnp.where(axis_ids >= i * width, values[i], chosen)
    return chosen


def chunks_of(width):
    unit = width // sum(SHARES)
    spans, at = [], 0
    for share in SHARES:
        spans.append((at, share * unit))
        at += share * unit
    return spans


def kernel(
    n_ctx, n_exp, counts, reach, tokens, keys, first, second, out,
    tokens_v, keys_v, first_v, second_v, normed, logits, weights, slot_in, send, recv, prod, outs, place,
    mix_own, mix_peer, placed_own, placed_peer, part_send, part_recv, summed, facts, facts_s,
    token_sem, key_sem, weight_sem, send_in, recv_in, send_own, recv_own, send_next, recv_next,
    send_mix, recv_mix, send_part, recv_part, send_facts, recv_facts, facts_sem,
):
    toks, width = tokens.shape
    slots = keys.shape[1]
    local = first.shape[0]
    hidden = first.shape[2]
    experts = counts.shape[1]
    levels = reach.shape[1]
    cap = 2 * slots // experts
    reach_width = slots // levels
    pairs = n_exp // 2
    mine_rows = local * cap
    half = pairs * mine_rows
    spans = chunks_of(width)
    ctx, me = lax.axis_index("ctx"), lax.axis_index("exp")
    side, pair = lax.rem(me, 2), me // 2
    window = ctx * n_exp + me
    windows = n_ctx * n_exp
    partner = me + 1 - 2 * side

    def device(number):
        number = lax.rem(number + windows, windows)
        return number // n_exp, lax.rem(number, n_exp)

    def exists(number):
        return jnp.logical_and(number >= 0, number < windows)

    def greet(barrier, where):
        pl.semaphore_signal(barrier, inc=1, device_id=where, device_id_type=MESH)

    piece = toks // HALVES
    token_loads = []
    for h in range(HALVES):
        rows = pl.ds(h * piece, piece)
        token_loads.append(pltpu.make_async_copy(tokens.at[rows], tokens_v.at[rows], token_sem.at[h]))
    key_load = pltpu.make_async_copy(keys, keys_v, key_sem)
    for load in token_loads:
        load.start()
    key_load.start()

    facts[...] = jnp.zeros(facts.shape, jnp.int32)
    barrier = pltpu.get_barrier_semaphore()
    for o in range(1, n_exp):
        greet(barrier, (ctx, lax.rem(me + o, n_exp)))
    for o in (-2, -1, 1):
        @pl.when(exists(window + o))
        def _(o=o):
            greet(barrier, device(window + o))

    @pl.when(jnp.logical_and(pair == 0, ctx > 0))
    def _():
        for i in range(pairs):
            greet(barrier, (ctx - 1, 2 * i + side))

    lane = iota((8, LANES), 1)
    row_facts = jnp.zeros((8, LANES), jnp.int32)
    for e in range(experts):
        row_facts = jnp.where(lane == e, counts[0, e], row_facts)
    for b in range(levels):
        row_facts = jnp.where(lane == experts + b, reach[0, b], row_facts)
    facts[0] = row_facts

    def normalize(at):
        rows = slice(at, at + ROWS)
        floats = tokens_v[rows, :].astype(jnp.float32)
        scale = lax.rsqrt(jnp.mean(floats * floats, axis=-1, keepdims=True) + EPSILON)
        normed[rows, :] = (floats * scale).astype(jnp.bfloat16)

    for h in range(HALVES):
        token_loads[h].wait()
        for at in range(h * piece, (h + 1) * piece, ROWS):
            normalize(at)
        if h == 0:
            key_load.wait()
        rows = slice(h * piece, (h + 1) * piece)
        logits[rows, :] = dot(normed[rows, :], keys_v[...])

    loads = []
    for j in range(local):
        for source, target, n in ((first, first_v, 0), (second, second_v, 1)):
            load = pltpu.make_async_copy(source.at[j], target.at[j], weight_sem.at[j, n])
            load.start()
            loads.append(load)

    slot_level = pick(iota((1, slots), 1), reach_width, [reach[0, b] for b in range(levels)])
    for b in range(slots // 128):
        cols = slice(b * 128, (b + 1) * 128)
        allowed = iota((toks, 128), 0) // BLOCK <= slot_level[:, cols]
        masked = jnp.where(allowed, logits[:, cols], -jnp.inf)
        exponent = jnp.exp(masked - jnp.max(masked, axis=0, keepdims=True))
        weights[:, cols] = (exponent / jnp.sum(exponent, axis=0, keepdims=True)).astype(jnp.bfloat16)
    slot_in[...] = lax.dot_general(
        weights[...], normed[...], (((0,), (0,)), ((), ())), preferred_element_type=jnp.float32
    ).astype(jnp.bfloat16)

    def starts_of(taken):
        starts, total = [], jnp.int32(0)
        for e in range(experts):
            starts.append(total)
            total = total + taken[e]
        return starts

    taken = [counts[0, e] for e in range(experts)]
    starts = starts_of(taken)

    told = sum(jnp.where(exists(window + o), 1, 0) for o in OFFSETS)
    pl.semaphore_wait(barrier, n_exp - 1 + told + jnp.where(ctx < n_ctx - 1, 1, 0))

    group = n_exp * cap
    mine = pl.ds(pl.multiple_of(me * cap, cap), cap)

    def tell(i, offset):
        return pltpu.make_async_remote_copy(
            src_ref=facts.at[0],
            dst_ref=facts.at[1 + i],
            send_sem=send_facts.at[i],
            recv_sem=recv_facts.at[i],
            device_id=device(window + offset),
            device_id_type=MESH,
        )

    for i, offset in enumerate(OFFSETS):
        @pl.when(exists(window + offset))
        def _(i=i, offset=offset):
            tell(i, offset).start()

    def to_expert(j, o):
        peer = lax.rem(me + o, n_exp)
        theirs = pl.ds(pl.multiple_of(peer * cap, cap), cap)
        return pltpu.make_async_remote_copy(
            src_ref=send.at[j, theirs],
            dst_ref=recv.at[j, mine],
            send_sem=send_in.at[j, o],
            recv_sem=recv_in.at[j, o],
            device_id=(ctx, peer),
            device_id_type=MESH,
        )

    for j in range(local):
        chosen = [d * local + j for d in range(n_exp)]
        row = iota((group, 1), 0)
        shift = pick(row, cap, [starts[e] - d * cap for d, e in enumerate(chosen)])
        limit = pick(row, cap, [taken[e] + d * cap for d, e in enumerate(chosen)])
        source = jnp.where(row < limit, row + shift, -1)
        hot = jnp.where(iota((group, slots), 1) == source, 1.0, 0.0).astype(jnp.bfloat16)
        send[j] = dot(hot, slot_in[...]).astype(jnp.bfloat16)
        for o in range(1, n_exp):
            to_expert(j, o).start()
        recv[j, mine, :] = send[j, mine, :]

    has_prior = window > 0

    def mixing(i, carry):
        rows = pl.ds(pl.multiple_of(i * ROWS, ROWS), ROWS)
        level = (iota((ROWS, slots), 0) + i * ROWS) // BLOCK
        allowed = slot_level <= level
        usable = jnp.logical_or(allowed, has_prior)
        masked = jnp.where(usable, logits[rows, :], -jnp.inf)
        every = jnp.exp(masked - jnp.max(masked, axis=1, keepdims=True))
        own = jnp.where(allowed, every, 0.0)
        prior = jnp.where(has_prior, every, 0.0)
        denominator = jnp.sum(own + prior, axis=1, keepdims=True)
        mix_own[rows, :] = (every / denominator).astype(jnp.bfloat16)
        return carry

    lax.fori_loop(0, toks // ROWS, mixing, 0)

    def to_partner(h):
        rows = pl.ds(h * piece, piece)
        return pltpu.make_async_remote_copy(
            src_ref=mix_own.at[rows],
            dst_ref=mix_peer.at[rows],
            send_sem=send_mix.at[h],
            recv_sem=recv_mix.at[h],
            device_id=(ctx, partner),
            device_id_type=MESH,
        )

    for h in range(HALVES):
        to_partner(h).start()

    for i, offset in enumerate(OFFSETS):
        @pl.when(exists(window - offset))
        def _(i=i, offset=offset):
            tell(i, offset).wait_recv()
    fetch = pltpu.make_async_copy(facts, facts_s, facts_sem)
    fetch.start()
    fetch.wait()

    odd = side == 1
    around = {0: 0, 1: 1, -1: 2, -2: 3}
    for t in range(3):
        seen = [
            jnp.where(odd, facts_s[around[t - 2], 0, e], facts_s[around[t - 1], 0, e])
            for e in range(experts)
        ]
        begin = starts_of(seen)
        column = iota((1, half), 1)
        shifts, limits = [], []
        for b in range(pairs * local):
            i, j = b // local, b % local
            even_e, odd_e = 2 * i * local + j, (2 * i + 1) * local + j
            shifts.append(jnp.where(odd, begin[odd_e], begin[even_e]) - b * cap)
            limits.append(jnp.where(odd, seen[odd_e], seen[even_e]) + b * cap)
        source = jnp.where(column < pick(column, cap, limits), column + pick(column, cap, shifts), -1)
        place[t] = jnp.where(iota((slots, half), 0) == source, 1.0, 0.0).astype(jnp.bfloat16)

    def settle(h, mix, placed, prior_place, own_place, level_of_slot, some_prior):
        rows = slice(h * piece, (h + 1) * piece)
        allowed = level_of_slot <= (iota((piece, slots), 0) + h * piece) // BLOCK
        every = mix[rows, :]
        prior = jnp.where(some_prior, dot(every, place[prior_place]), 0.0)
        placed[rows, :half] = prior.astype(jnp.bfloat16)
        own = jnp.where(allowed, every.astype(jnp.float32), 0.0).astype(jnp.bfloat16)
        placed[rows, half:] = dot(own, place[own_place]).astype(jnp.bfloat16)

    for h in range(HALVES):
        settle(h, mix_own, placed_own, side, 1 + side, slot_level, has_prior)
    peer_level = pick(
        iota((1, slots), 1), reach_width,
        [jnp.where(odd, facts_s[2, 0, experts + b], facts_s[1, 0, experts + b]) for b in range(levels)],
    )

    home_rows = pl.ds(pl.multiple_of(pair * mine_rows, mine_rows), mine_rows)

    def returns(unit, rows, span, o, t):
        target = lax.rem(pair + o, pairs)
        cols = pl.ds(*span)
        there = pl.ds(pl.multiple_of(pair * mine_rows + rows[0], cap), rows[1])
        return pltpu.make_async_remote_copy(
            src_ref=prod.at[2 * target + t, pl.ds(*rows), cols],
            dst_ref=outs.at[1 + t, there, cols],
            send_sem=send_own.at[unit, o, t],
            recv_sem=recv_own.at[unit, o, t],
            device_id=(ctx, 2 * target + side),
            device_id_type=MESH,
        )

    def to_next(unit, rows, span, o):
        target = lax.rem(pair + o, pairs)
        cols = pl.ds(*span)
        there = pl.ds(pl.multiple_of(pair * mine_rows + rows[0], cap), rows[1])
        later = jnp.where(target == 0, 1, 0)
        return pltpu.make_async_remote_copy(
            src_ref=prod.at[lax.rem(2 * target + n_exp - 1, n_exp), pl.ds(*rows), cols],
            dst_ref=outs.at[0, there, cols],
            send_sem=send_next.at[unit, o],
            recv_sem=recv_next.at[unit, o],
            device_id=(lax.rem(ctx + later, n_ctx), 2 * target + side),
            device_id_type=MESH,
        )

    def each_return(t, unit, rows, c, act):
        for o in range(1, pairs):
            act(returns(unit, rows, spans[c], o, t))

    more, earlier = ctx < n_ctx - 1, ctx > 0

    def each_next(unit, rows, c, act, arriving=False):
        for o in range(pairs):
            first_of = pair == 0 if arriving else lax.rem(pair + o, pairs) == 0
            across = jnp.logical_and(first_of, earlier if arriving else more)
            needed = across if o == 0 else jnp.logical_or(jnp.logical_not(first_of), across)

            @pl.when(needed)
            def _(o=o):
                act(to_next(unit, rows, spans[c], o))

    even, odd_side = side == 0, side == 1

    def begin(copy):
        copy.start()

    def send_back(unit, passed):
        @pl.when(even)
        def _():
            each_return(0, *unit, begin)
            each_return(1, *unit, begin)
            for other in passed[0]:
                each_next(*other, begin)

        @pl.when(odd_side)
        def _():
            for other in passed[1]:
                each_next(*other, begin)
            each_return(0, *unit, begin)
            each_return(1, *unit, begin)

    units = [(j, (j * cap, cap), 0) for j in range(local)]
    units += [(local + c - 1, (0, mine_rows), c) for c in range(1, len(spans))]

    tile = min(512, hidden)
    for j in range(local):
        loads[2 * j].wait()
        loads[2 * j + 1].wait()
        for o in range(1, n_exp):
            to_expert(j, o).wait_recv()
        total_out = None
        for t in range(hidden // tile):
            cols = slice(t * tile, (t + 1) * tile)
            active = jax.nn.gelu(dot(recv[j], first_v[j, :, cols]), approximate=True)
            term = dot(active.astype(jnp.bfloat16), second_v[j, cols, :])
            total_out = term if total_out is None else total_out + term
        prod[:, j * cap:(j + 1) * cap, :] = total_out.astype(jnp.bfloat16).reshape(n_exp, cap, width)
        send_back(units[j], (units[j:j + 1], units[j:j + 1]))
    whole = {c: (local + c - 1, (0, mine_rows), c) for c in range(1, len(spans))}
    send_back(whole[1], [[whole[c] for c in range(1, lead)] for lead in LEADS])

    outs[pl.ds(1, 2), home_rows, :] = prod[pl.ds(2 * pair, 2), :, :]

    @pl.when(pair > 0)
    def _():
        outs[0, home_rows, :] = prod[2 * pair - 1]

    @pl.when(jnp.logical_and(pair == 0, ctx == 0))
    def _():
        outs[0] = jnp.zeros(outs.shape[1:], jnp.bfloat16)

    shares = [(c, h * piece, piece) for c in range(1) for h in range(HALVES)]
    shares += [(c, 0, toks) for c in range(1, len(spans))]

    def share(n):
        c, at, size = shares[n]
        rows, cols = pl.ds(at, size), pl.ds(*spans[c])
        return pltpu.make_async_remote_copy(
            src_ref=part_send.at[rows, cols],
            dst_ref=part_recv.at[rows, cols],
            send_sem=send_part.at[n],
            recv_sem=recv_part.at[n],
            device_id=(ctx, partner),
            device_id_type=MESH,
        )

    def returned(c, t):
        for unit in units:
            if unit[2] == c:
                if t > 0:
                    each_return(t - 1, *unit, lambda copy: copy.wait_recv())
                else:
                    each_next(*unit, lambda copy: copy.wait_recv(), arriving=True)

    for n, (c, at, size) in enumerate(shares):
        cols = slice(spans[c][0], spans[c][0] + spans[c][1])
        rows = slice(at, at + size)
        if at == 0:
            returned(c, 1)

            @pl.when(even)
            def _(c=c):
                returned(c, 2)

            @pl.when(odd_side)
            def _(c=c):
                returned(c, 0)

            passed = [[whole[c + lead]] if c + lead < len(spans) else [] for lead in LEADS]
            if c + 2 < len(spans):
                send_back(whole[c + 2], passed)
            elif passed[0]:
                @pl.when(even)
                def _(c=c):
                    each_next(*whole[c + LEADS[0]], begin)
        if c == 0:
            to_partner(n).wait_recv()
            settle(
                n, mix_peer, placed_peer, 1 - side, 2 - side, peer_level,
                ctx * n_exp + partner > 0,
            )
        theirs = outs[pl.ds(1 - side, 2), :, cols].reshape(2 * half, spans[c][1])
        part_send[rows, cols] = dot(placed_peer[rows, :], theirs).astype(jnp.bfloat16)
        share(n).start()
        if at + size == toks:
            @pl.when(even)
            def _(c=c):
                returned(c, 0)

            @pl.when(odd_side)
            def _(c=c):
                returned(c, 2)

            ours = outs[pl.ds(side, 2), :, cols].reshape(2 * half, spans[c][1])
            summed[:, cols] = dot(placed_own[...], ours)

    for n, (c, at, size) in enumerate(shares):
        share(n).wait_recv()
        cols = slice(spans[c][0], spans[c][0] + spans[c][1])
        rows = slice(at, at + size)
        received = part_recv[rows, cols].astype(jnp.float32)
        out[rows, cols] = (summed[rows, cols] + received).astype(jnp.bfloat16)

    for i, offset in enumerate(OFFSETS):
        @pl.when(exists(window + offset))
        def _(i=i, offset=offset):
            tell(i, offset).wait_send()
    for h in range(HALVES):
        to_partner(h).wait_send()
    for n in range(len(shares)):
        share(n).wait_send()
    for unit in units:
        each_return(0, *unit, lambda copy: copy.wait_send())
        each_return(1, *unit, lambda copy: copy.wait_send())
        each_next(*unit, lambda copy: copy.wait_send())
    for j in range(local):
        for o in range(1, n_exp):
            to_expert(j, o).wait_send()


def layer(n_ctx, n_exp, tokens, slot_keys, expert_in, expert_out, slot_counts, slot_reach):
    toks, width = tokens.shape
    slots = slot_keys.shape[1]
    local = expert_in.shape[0]
    experts = slot_counts.shape[1]
    cap = 2 * slots // experts
    pairs = n_exp // 2
    half = pairs * local * cap
    units = local + len(SHARES) - 1
    bf16, f32 = jnp.bfloat16, jnp.float32
    in_vmem = pl.BlockSpec(memory_space=pltpu.VMEM)
    in_smem = pl.BlockSpec(memory_space=pltpu.SMEM)
    in_any = pl.BlockSpec(memory_space=pl.ANY)
    dma = pltpu.SemaphoreType.DMA
    return pl.pallas_call(
        functools.partial(kernel, n_ctx, n_exp),
        out_shape=pltpu.VMEM((toks, width), bf16),
        in_specs=[in_smem, in_smem, in_any, in_any, in_any, in_any],
        out_specs=in_vmem,
        scratch_shapes=[
            pltpu.VMEM((toks, width), bf16),
            pltpu.VMEM(slot_keys.shape, bf16),
            pltpu.VMEM(expert_in.shape, bf16),
            pltpu.VMEM(expert_out.shape, bf16),
            pltpu.VMEM((toks, width), bf16),
            pltpu.VMEM((toks, slots), f32),
            pltpu.VMEM((toks, slots), bf16),
            pltpu.VMEM((slots, width), bf16),
            pltpu.VMEM((local, n_exp * cap, width), bf16),
            pltpu.VMEM((local, n_exp * cap, width), bf16),
            pltpu.VMEM((n_exp, local * cap, width), bf16),
            pltpu.VMEM((3, half, width), bf16),
            pltpu.VMEM((3, slots, half), bf16),
            pltpu.VMEM((toks, slots), bf16),
            pltpu.VMEM((toks, slots), bf16),
            pltpu.VMEM((toks, 2 * half), bf16),
            pltpu.VMEM((toks, 2 * half), bf16),
            pltpu.VMEM((toks, width), bf16),
            pltpu.VMEM((toks, width), bf16),
            pltpu.VMEM((toks, width), f32),
            pltpu.VMEM((4, 8, LANES), jnp.int32),
            pltpu.SMEM((4, 8, LANES), jnp.int32),
            dma((HALVES,)),
            dma,
            dma((local, 2)),
            dma((local, n_exp)),
            dma((local, n_exp)),
            dma((units, pairs, 2)),
            dma((units, pairs, 2)),
            dma((units, pairs)),
            dma((units, pairs)),
            dma((HALVES,)),
            dma((HALVES,)),
            dma((len(SHARES) + HALVES,)),
            dma((len(SHARES) + HALVES,)),
            dma((3,)),
            dma((3,)),
            dma,
        ],
        compiler_params=pltpu.CompilerParams(
            collective_id=0, has_side_effects=True, vmem_limit_bytes=60*2**20
        ),
    )(slot_counts, slot_reach, tokens, slot_keys, expert_in, expert_out)


def solution(mesh):
    placed = (
        P(("ctx", "exp"), None),
        P(),
        P("exp", None, None),
        P("exp", None, None),
        P(("ctx", "exp"), None),
        P(("ctx", "exp"), None),
    )
    body = functools.partial(layer, mesh.shape["ctx"], mesh.shape["exp"])
    return jax.shard_map(
        body, mesh=mesh, in_specs=placed, out_specs=P(("ctx", "exp"), None), check_vma=False
    )
```

```python
import functools

import jax
import jax.numpy as jnp
from jax import lax
from jax.experimental import pallas as pl
from jax.experimental.pallas import tpu as pltpu
from jax.sharding import PartitionSpec as P

BLOCK = 64
EPSILON = 1e-06
MESH = pl.DeviceIdType.MESH
ROWS = 64
LANES = 128
SHARES = (2, 1, 1, 1, 1, 1, 1)
HALVES = 2
LEADS = (3, 5)
OFFSETS = (-1, 1, 2)


def iota(shape, dim):
    return lax.broadcasted_iota(jnp.int32, shape, dim)


def dot(a, b):
    return jnp.dot(a, b, preferred_element_type=jnp.float32)


def pick(axis_ids, width, values):
    chosen = jnp.full(axis_ids.shape, values[0], jnp.int32)
    for i in range(1, len(values)):
        chosen = jnp.where(axis_ids >= i * width, values[i], chosen)
    return chosen


def chunks_of(width):
    unit = width // sum(SHARES)
    spans, at = [], 0
    for share in SHARES:
        spans.append((at, share * unit))
        at += share * unit
    return spans


def kernel(
    n_ctx, n_exp, counts, reach, tokens, keys, first, second, out,
    tokens_v, keys_v, first_v, second_v, normed, logits, weights, slot_in, send, recv, prod, outs, place,
    mix_own, mix_peer, placed_own, placed_peer, part_send, part_recv, summed, facts, facts_s,
    token_sem, key_sem, weight_sem, send_in, recv_in, send_own, recv_own, send_next, recv_next,
    send_mix, recv_mix, send_part, recv_part, send_facts, recv_facts, facts_sem,
):
    toks, width = tokens.shape
    slots = keys.shape[1]
    local = first.shape[0]
    hidden = first.shape[2]
    experts = counts.shape[1]
    levels = reach.shape[1]
    cap = 2 * slots // experts
    reach_width = slots // levels
    pairs = n_exp // 2
    mine_rows = local * cap
    half = pairs * mine_rows
    spans = chunks_of(width)
    ctx, me = lax.axis_index("ctx"), lax.axis_index("exp")
    side, pair = lax.rem(me, 2), me // 2
    window = ctx * n_exp + me
    windows = n_ctx * n_exp
    partner = me + 1 - 2 * side

    def device(number):
        number = lax.rem(number + windows, windows)
        return number // n_exp, lax.rem(number, n_exp)

    def exists(number):
        return jnp.logical_and(number >= 0, number < windows)

    def greet(barrier, where):
        pl.semaphore_signal(barrier, inc=1, device_id=where, device_id_type=MESH)

    facts[...] = jnp.zeros(facts.shape, jnp.int32)
    barrier = pltpu.get_barrier_semaphore()
    for o in range(1, n_exp):
        greet(barrier, (ctx, lax.rem(me + o, n_exp)))
    for o in (-2, -1, 1):
        @pl.when(exists(window + o))
        def _(o=o):
            greet(barrier, device(window + o))

    @pl.when(jnp.logical_and(pair == 0, ctx > 0))
    def _():
        for i in range(pairs):
            greet(barrier, (ctx - 1, 2 * i + side))

    piece = toks // HALVES
    token_loads = []
    for h in range(HALVES):
        rows = pl.ds(h * piece, piece)
        token_loads.append(pltpu.make_async_copy(tokens.at[rows], tokens_v.at[rows], token_sem.at[h]))
    key_load = pltpu.make_async_copy(keys, keys_v, key_sem)
    for load in token_loads:
        load.start()
    key_load.start()

    lane = iota((8, LANES), 1)
    row_facts = jnp.zeros((8, LANES), jnp.int32)
    for e in range(experts):
        row_facts = jnp.where(lane == e, counts[0, e], row_facts)
    for b in range(levels):
        row_facts = jnp.where(lane == experts + b, reach[0, b], row_facts)
    facts[0] = row_facts

    def normalize(at):
        rows = slice(at, at + ROWS)
        floats = tokens_v[rows, :].astype(jnp.float32)
        scale = lax.rsqrt(jnp.mean(floats * floats, axis=-1, keepdims=True) + EPSILON)
        normed[rows, :] = (floats * scale).astype(jnp.bfloat16)

    for h in range(HALVES):
        token_loads[h].wait()
        for at in range(h * piece, (h + 1) * piece, ROWS):
            normalize(at)
        if h == 0:
            key_load.wait()
        rows = slice(h * piece, (h + 1) * piece)
        logits[rows, :] = dot(normed[rows, :], keys_v[...])

    loads = []
    for j in range(local):
        for source, target, n in ((first, first_v, 0), (second, second_v, 1)):
            load = pltpu.make_async_copy(source.at[j], target.at[j], weight_sem.at[j, n])
            load.start()
            loads.append(load)

    slot_level = pick(iota((1, slots), 1), reach_width, [reach[0, b] for b in range(levels)])
    for b in range(slots // 128):
        cols = slice(b * 128, (b + 1) * 128)
        allowed = iota((toks, 128), 0) // BLOCK <= slot_level[:, cols]
        masked = jnp.where(allowed, logits[:, cols], -jnp.inf)
        exponent = jnp.exp(masked - jnp.max(masked, axis=0, keepdims=True))
        weights[:, cols] = (exponent / jnp.sum(exponent, axis=0, keepdims=True)).astype(jnp.bfloat16)
    slot_in[...] = lax.dot_general(
        weights[...], normed[...], (((0,), (0,)), ((), ())), preferred_element_type=jnp.float32
    ).astype(jnp.bfloat16)

    def starts_of(taken):
        starts, total = [], jnp.int32(0)
        for e in range(experts):
            starts.append(total)
            total = total + taken[e]
        return starts

    taken = [counts[0, e] for e in range(experts)]
    starts = starts_of(taken)

    told = sum(jnp.where(exists(window + o), 1, 0) for o in OFFSETS)
    pl.semaphore_wait(barrier, n_exp - 1 + told + jnp.where(ctx < n_ctx - 1, 1, 0))

    group = n_exp * cap
    mine = pl.ds(pl.multiple_of(me * cap, cap), cap)

    def tell(i, offset):
        return pltpu.make_async_remote_copy(
            src_ref=facts.at[0],
            dst_ref=facts.at[1 + i],
            send_sem=send_facts.at[i],
            recv_sem=recv_facts.at[i],
            device_id=device(window + offset),
            device_id_type=MESH,
        )

    for i, offset in enumerate(OFFSETS):
        @pl.when(exists(window + offset))
        def _(i=i, offset=offset):
            tell(i, offset).start()

    def to_expert(j, o):
        peer = lax.rem(me + o, n_exp)
        theirs = pl.ds(pl.multiple_of(peer * cap, cap), cap)
        return pltpu.make_async_remote_copy(
            src_ref=send.at[j, theirs],
            dst_ref=recv.at[j, mine],
            send_sem=send_in.at[j, o],
            recv_sem=recv_in.at[j, o],
            device_id=(ctx, peer),
            device_id_type=MESH,
        )

    for j in range(local):
        chosen = [d * local + j for d in range(n_exp)]
        row = iota((group, 1), 0)
        shift = pick(row, cap, [starts[e] - d * cap for d, e in enumerate(chosen)])
        limit = pick(row, cap, [taken[e] + d * cap for d, e in enumerate(chosen)])
        source = jnp.where(row < limit, row + shift, -1)
        hot = jnp.where(iota((group, slots), 1) == source, 1.0, 0.0).astype(jnp.bfloat16)
        send[j] = dot(hot, slot_in[...]).astype(jnp.bfloat16)
        for o in range(1, n_exp):
            to_expert(j, o).start()
        recv[j, mine, :] = send[j, mine, :]

    has_prior = window > 0

    def mixing(i, carry):
        rows = pl.ds(pl.multiple_of(i * ROWS, ROWS), ROWS)
        level = (iota((ROWS, slots), 0) + i * ROWS) // BLOCK
        allowed = slot_level <= level
        usable = jnp.logical_or(allowed, has_prior)
        masked = jnp.where(usable, logits[rows, :], -jnp.inf)
        every = jnp.exp(masked - jnp.max(masked, axis=1, keepdims=True))
        own = jnp.where(allowed, every, 0.0)
        prior = jnp.where(has_prior, every, 0.0)
        denominator = jnp.sum(own + prior, axis=1, keepdims=True)
        mix_own[rows, :] = (every / denominator).astype(jnp.bfloat16)
        return carry

    lax.fori_loop(0, toks // ROWS, mixing, 0)

    def to_partner(h):
        rows = pl.ds(h * piece, piece)
        return pltpu.make_async_remote_copy(
            src_ref=mix_own.at[rows],
            dst_ref=mix_peer.at[rows],
            send_sem=send_mix.at[h],
            recv_sem=recv_mix.at[h],
            device_id=(ctx, partner),
            device_id_type=MESH,
        )

    for h in range(HALVES):
        to_partner(h).start()

    for i, offset in enumerate(OFFSETS):
        @pl.when(exists(window - offset))
        def _(i=i, offset=offset):
            tell(i, offset).wait_recv()
    fetch = pltpu.make_async_copy(facts, facts_s, facts_sem)
    fetch.start()
    fetch.wait()

    odd = side == 1
    around = {0: 0, 1: 1, -1: 2, -2: 3}
    for t in range(3):
        seen = [
            jnp.where(odd, facts_s[around[t - 2], 0, e], facts_s[around[t - 1], 0, e])
            for e in range(experts)
        ]
        begin = starts_of(seen)
        column = iota((1, half), 1)
        shifts, limits = [], []
        for b in range(pairs * local):
            i, j = b // local, b % local
            even_e, odd_e = 2 * i * local + j, (2 * i + 1) * local + j
            shifts.append(jnp.where(odd, begin[odd_e], begin[even_e]) - b * cap)
            limits.append(jnp.where(odd, seen[odd_e], seen[even_e]) + b * cap)
        source = jnp.where(column < pick(column, cap, limits), column + pick(column, cap, shifts), -1)
        place[t] = jnp.where(iota((slots, half), 0) == source, 1.0, 0.0).astype(jnp.bfloat16)

    def settle(h, mix, placed, prior_place, own_place, level_of_slot, some_prior):
        rows = slice(h * piece, (h + 1) * piece)
        allowed = level_of_slot <= (iota((piece, slots), 0) + h * piece) // BLOCK
        every = mix[rows, :]
        prior = jnp.where(some_prior, dot(every, place[prior_place]), 0.0)
        placed[rows, :half] = prior.astype(jnp.bfloat16)
        own = jnp.where(allowed, every.astype(jnp.float32), 0.0).astype(jnp.bfloat16)
        placed[rows, half:] = dot(own, place[own_place]).astype(jnp.bfloat16)

    for h in range(HALVES):
        settle(h, mix_own, placed_own, side, 1 + side, slot_level, has_prior)
    peer_level = pick(
        iota((1, slots), 1), reach_width,
        [jnp.where(odd, facts_s[2, 0, experts + b], facts_s[1, 0, experts + b]) for b in range(levels)],
    )

    home_rows = pl.ds(pl.multiple_of(pair * mine_rows, mine_rows), mine_rows)

    def returns(unit, rows, span, o, t):
        target = lax.rem(pair + o, pairs)
        cols = pl.ds(*span)
        there = pl.ds(pl.multiple_of(pair * mine_rows + rows[0], cap), rows[1])
        return pltpu.make_async_remote_copy(
            src_ref=prod.at[2 * target + t, pl.ds(*rows), cols],
            dst_ref=outs.at[1 + t, there, cols],
            send_sem=send_own.at[unit, o, t],
            recv_sem=recv_own.at[unit, o, t],
            device_id=(ctx, 2 * target + side),
            device_id_type=MESH,
        )

    def to_next(unit, rows, span, o):
        target = lax.rem(pair + o, pairs)
        cols = pl.ds(*span)
        there = pl.ds(pl.multiple_of(pair * mine_rows + rows[0], cap), rows[1])
        later = jnp.where(target == 0, 1, 0)
        return pltpu.make_async_remote_copy(
            src_ref=prod.at[lax.rem(2 * target + n_exp - 1, n_exp), pl.ds(*rows), cols],
            dst_ref=outs.at[0, there, cols],
            send_sem=send_next.at[unit, o],
            recv_sem=recv_next.at[unit, o],
            device_id=(lax.rem(ctx + later, n_ctx), 2 * target + side),
            device_id_type=MESH,
        )

    def each_return(t, unit, rows, c, act):
        for o in range(1, pairs):
            act(returns(unit, rows, spans[c], o, t))

    more, earlier = ctx < n_ctx - 1, ctx > 0

    def each_next(unit, rows, c, act, arriving=False):
        for o in range(pairs):
            first_of = pair == 0 if arriving else lax.rem(pair + o, pairs) == 0
            across = jnp.logical_and(first_of, earlier if arriving else more)
            needed = across if o == 0 else jnp.logical_or(jnp.logical_not(first_of), across)

            @pl.when(needed)
            def _(o=o):
                act(to_next(unit, rows, spans[c], o))

    even, odd_side = side == 0, side == 1

    def begin(copy):
        copy.start()

    def send_back(unit, passed):
        @pl.when(even)
        def _():
            each_return(0, *unit, begin)
            each_return(1, *unit, begin)
            for other in passed[0]:
                each_next(*other, begin)

        @pl.when(odd_side)
        def _():
            for other in passed[1]:
                each_next(*other, begin)
            each_return(0, *unit, begin)
            each_return(1, *unit, begin)

    units = [(j, (j * cap, cap), 0) for j in range(local)]
    units += [(local + c - 1, (0, mine_rows), c) for c in range(1, len(spans))]

    tile = min(1024, hidden)
    for j in range(local):
        loads[2 * j].wait()
        loads[2 * j + 1].wait()
        for o in range(1, n_exp):
            to_expert(j, o).wait_recv()
        total_out = None
        for t in range(hidden // tile):
            cols = slice(t * tile, (t + 1) * tile)
            active = jax.nn.gelu(dot(recv[j], first_v[j, :, cols]), approximate=True)
            term = dot(active.astype(jnp.bfloat16), second_v[j, cols, :])
            total_out = term if total_out is None else total_out + term
        prod[:, j * cap:(j + 1) * cap, :] = total_out.astype(jnp.bfloat16).reshape(n_exp, cap, width)
        send_back(units[j], (units[j:j + 1], units[j:j + 1]))
    whole = {c: (local + c - 1, (0, mine_rows), c) for c in range(1, len(spans))}
    send_back(whole[1], [[whole[c] for c in range(1, lead)] for lead in LEADS])

    outs[pl.ds(1, 2), home_rows, :] = prod[pl.ds(2 * pair, 2), :, :]

    @pl.when(pair > 0)
    def _():
        outs[0, home_rows, :] = prod[2 * pair - 1]

    @pl.when(jnp.logical_and(pair == 0, ctx == 0))
    def _():
        outs[0] = jnp.zeros(outs.shape[1:], jnp.bfloat16)

    shares = [(c, h * piece, piece) for c in range(1) for h in range(HALVES)]
    shares += [(c, 0, toks) for c in range(1, len(spans) - 1)]
    shares += [(len(spans) - 1, h * piece, piece) for h in range(HALVES)]

    def share(n):
        c, at, size = shares[n]
        rows, cols = pl.ds(at, size), pl.ds(*spans[c])
        return pltpu.make_async_remote_copy(
            src_ref=part_send.at[rows, cols],
            dst_ref=part_recv.at[rows, cols],
            send_sem=send_part.at[n],
            recv_sem=recv_part.at[n],
            device_id=(ctx, partner),
            device_id_type=MESH,
        )

    def returned(c, t):
        for unit in units:
            if unit[2] == c:
                if t > 0:
                    each_return(t - 1, *unit, lambda copy: copy.wait_recv())
                else:
                    each_next(*unit, lambda copy: copy.wait_recv(), arriving=True)

    for n, (c, at, size) in enumerate(shares):
        cols = slice(spans[c][0], spans[c][0] + spans[c][1])
        rows = slice(at, at + size)
        if at == 0:
            returned(c, 1)

            @pl.when(even)
            def _(c=c):
                returned(c, 2)

            @pl.when(odd_side)
            def _(c=c):
                returned(c, 0)

            passed = [[whole[c + lead]] if c + lead < len(spans) else [] for lead in LEADS]
            if c + 2 < len(spans):
                send_back(whole[c + 2], passed)
            elif passed[0]:
                @pl.when(even)
                def _(c=c):
                    each_next(*whole[c + LEADS[0]], begin)
        if c == 0:
            to_partner(n).wait_recv()
            settle(
                n, mix_peer, placed_peer, 1 - side, 2 - side, peer_level,
                ctx * n_exp + partner > 0,
            )
        theirs = outs[pl.ds(1 - side, 2), :, cols].reshape(2 * half, spans[c][1])
        part_send[rows, cols] = dot(placed_peer[rows, :], theirs).astype(jnp.bfloat16)
        share(n).start()
        if at + size == toks:
            @pl.when(even)
            def _(c=c):
                returned(c, 0)

            @pl.when(odd_side)
            def _(c=c):
                returned(c, 2)

            ours = outs[pl.ds(side, 2), :, cols].reshape(2 * half, spans[c][1])
            summed[:, cols] = dot(placed_own[...], ours)

    for n, (c, at, size) in enumerate(shares):
        share(n).wait_recv()
        cols = slice(spans[c][0], spans[c][0] + spans[c][1])
        rows = slice(at, at + size)
        received = part_recv[rows, cols].astype(jnp.float32)
        out[rows, cols] = (summed[rows, cols] + received).astype(jnp.bfloat16)

    for i, offset in enumerate(OFFSETS):
        @pl.when(exists(window + offset))
        def _(i=i, offset=offset):
            tell(i, offset).wait_send()
    for h in range(HALVES):
        to_partner(h).wait_send()
    for n in range(len(shares)):
        share(n).wait_send()
    for unit in units:
        each_return(0, *unit, lambda copy: copy.wait_send())
        each_return(1, *unit, lambda copy: copy.wait_send())
        each_next(*unit, lambda copy: copy.wait_send())
    for j in range(local):
        for o in range(1, n_exp):
            to_expert(j, o).wait_send()


def layer(n_ctx, n_exp, tokens, slot_keys, expert_in, expert_out, slot_counts, slot_reach):
    toks, width = tokens.shape
    slots = slot_keys.shape[1]
    local = expert_in.shape[0]
    experts = slot_counts.shape[1]
    cap = 2 * slots // experts
    pairs = n_exp // 2
    half = pairs * local * cap
    units = local + len(SHARES) - 1
    bf16, f32 = jnp.bfloat16, jnp.float32
    in_vmem = pl.BlockSpec(memory_space=pltpu.VMEM)
    in_smem = pl.BlockSpec(memory_space=pltpu.SMEM)
    in_any = pl.BlockSpec(memory_space=pl.ANY)
    dma = pltpu.SemaphoreType.DMA
    return pl.pallas_call(
        functools.partial(kernel, n_ctx, n_exp),
        out_shape=pltpu.VMEM((toks, width), bf16),
        in_specs=[in_smem, in_smem, in_any, in_any, in_any, in_any],
        out_specs=in_vmem,
        scratch_shapes=[
            pltpu.VMEM((toks, width), bf16),
            pltpu.VMEM(slot_keys.shape, bf16),
            pltpu.VMEM(expert_in.shape, bf16),
            pltpu.VMEM(expert_out.shape, bf16),
            pltpu.VMEM((toks, width), bf16),
            pltpu.VMEM((toks, slots), f32),
            pltpu.VMEM((toks, slots), bf16),
            pltpu.VMEM((slots, width), bf16),
            pltpu.VMEM((local, n_exp * cap, width), bf16),
            pltpu.VMEM((local, n_exp * cap, width), bf16),
            pltpu.VMEM((n_exp, local * cap, width), bf16),
            pltpu.VMEM((3, half, width), bf16),
            pltpu.VMEM((3, slots, half), bf16),
            pltpu.VMEM((toks, slots), bf16),
            pltpu.VMEM((toks, slots), bf16),
            pltpu.VMEM((toks, 2 * half), bf16),
            pltpu.VMEM((toks, 2 * half), bf16),
            pltpu.VMEM((toks, width), bf16),
            pltpu.VMEM((toks, width), bf16),
            pltpu.VMEM((toks, width), f32),
            pltpu.VMEM((4, 8, LANES), jnp.int32),
            pltpu.SMEM((4, 8, LANES), jnp.int32),
            dma((HALVES,)),
            dma,
            dma((local, 2)),
            dma((local, n_exp)),
            dma((local, n_exp)),
            dma((units, pairs, 2)),
            dma((units, pairs, 2)),
            dma((units, pairs)),
            dma((units, pairs)),
            dma((HALVES,)),
            dma((HALVES,)),
            dma((len(SHARES) + HALVES,)),
            dma((len(SHARES) + HALVES,)),
            dma((3,)),
            dma((3,)),
            dma,
        ],
        compiler_params=pltpu.CompilerParams(
            collective_id=0, has_side_effects=True, vmem_limit_bytes=60*2**20
        ),
    )(slot_counts, slot_reach, tokens, slot_keys, expert_in, expert_out)


def solution(mesh):
    placed = (
        P(("ctx", "exp"), None),
        P(),
        P("exp", None, None),
        P("exp", None, None),
        P(("ctx", "exp"), None),
        P(("ctx", "exp"), None),
    )
    body = functools.partial(layer, mesh.shape["ctx"], mesh.shape["exp"])
    return jax.shard_map(
        body, mesh=mesh, in_specs=placed, out_specs=P(("ctx", "exp"), None), check_vma=False
    )
```
